32 devices in a mesh: tens: 2 (over y), atom: 16 (over z, x, core).
Axes of the slice: x: 2, y: 2, z: 4, core: 2. Of those that a mesh axis runs over, the one named last changes fastest.
Arguments:
- chibar: float32 [96, 4096], P(None, 'atom'), may hold values from -6 to 6
- t_blocks: float32 [384, 196608], P(None, ('tens', 'atom')), may hold values from -0.3125 to 0.3125
- n_saved: float32 [96, 196608], P('tens', 'atom'), may hold values from -0.078125 to 0.078125
- q_list: int32 [2, 16, 3], P('tens', 'atom'), may hold values from 0 to 13, as said below
- q_count: int32 [2, 16], P('tens', 'atom'), may hold values from 1 to 3, as said below
Outputs:
- gbar: float32 [1024, 320], P('atom')
The draws below stay inside these ranges and needn't reach their ends.
Inputs may be any that keep to these rules, and one draw needn't show every extreme that they name: `q_list`: the 3 entries of one pair owner's list name blocks of 3 distinct atom indices. `q_count`: equal to 3 on at least one pair owner.
All inputs are finite; a program needn't handle non-finite values.
Results may differ from the reference program's by a relative error of at most 0.0003.
Values sent between devices are 32-bit elements; how exact they have to be, the bound alone decides.
No kernel may reach another device: no remote copies, remote signals or barrier semaphores. Data moves between devices by JAX's collectives and lax.ppermute only.
A program may use at most 64 MiB of HBM per device.

```python
import jax
import jax.numpy as jnp
from jax import lax

BLK = 128
ORB_DEV = 64
QB_DEV = 2
REACH = 3
QL = 3
P_WIN = 96
NAUX = 4096
NORB = 1024
NU_T = 96
PAIR_DEV = 6144
N_TENS = 2
N_ATOM = 16
DEVICES = 32


def draw_q_list(key, part):
    owners = N_TENS * N_ATOM
    keys = jax.random.split(jax.random.fold_in(key, 11), owners)
    atoms = jax.vmap(lambda single: jax.random.permutation(single, 2 * REACH + 1)[:QL])(keys)
    within = jax.random.randint(jax.random.fold_in(key, 12), (owners, QL), 0, QB_DEV)
    slots = atoms * QB_DEV + within
    return slots.reshape(N_TENS, N_ATOM, QL).astype(jnp.int32)


def draw_q_count(key, part):
    owners = N_TENS * N_ATOM
    counts = jax.random.randint(jax.random.fold_in(key, 21), (owners,), 1, QL + 1)
    chosen_owner = jax.random.randint(jax.random.fold_in(key, 22), (), 0, owners)
    counts = jnp.where(jnp.arange(owners) == chosen_owner, QL, counts)
    return counts.reshape(N_TENS, N_ATOM).astype(jnp.int32)


def level_of(stream_key, extent, cuts, least, high):
    factor_of = 1.0
    for position, shards_of in cuts:
        draws = jax.random.uniform(jax.random.fold_in(jax.random.fold_in(stream_key, 6), position), (shards_of,), jnp.float32, least / len(cuts), high / len(cuts))
        factor_of = factor_of * jnp.repeat(jnp.exp(draws), extent[position] // shards_of).reshape((-1,) + (1,) * (len(extent) - 1 - position))
    return factor_of


def normal_values(stream_key, dims, deviation, reach, cuts=(), held_as=jnp.bfloat16):
    entries = deviation * jax.random.normal(stream_key, dims, jnp.float32)
    if cuts:
        entries = entries * level_of(stream_key, dims, cuts, -0.22, 0.18)
    return jnp.clip(entries, -reach, reach).astype(held_as)


def setup_inputs(seed: int = 0) -> dict:
    streams_of = jax.random.split(jax.random.key(seed), 6)
    chibar = normal_values(streams_of[0], (P_WIN, NAUX), 1.0, 6.0, ((1, 16),), jnp.float32)
    t_blocks = normal_values(streams_of[1], (QL * BLK, DEVICES * PAIR_DEV), (QL * BLK) ** -0.5, 0.3125, ((1, 32),), jnp.float32)
    n_saved = normal_values(streams_of[2], (P_WIN, NORB * 3 * ORB_DEV), (P_WIN * ORB_DEV) ** -0.5, 0.078125, ((0, 2), (1, 16)), jnp.float32)
    q_list = draw_q_list(jax.random.fold_in(streams_of[5], 71), 0)
    q_count = draw_q_count(jax.random.fold_in(streams_of[5], 71), 0)
    return {"chibar": chibar, "t_blocks": t_blocks, "n_saved": n_saved, "q_list": q_list, "q_count": q_count}


def place_block(block, offset, orb_width):
    return jnp.pad(block, ((0, 0), (0, 0), (offset * orb_width, (2 - offset) * orb_width)))


def reference(chibar, t_blocks, n_saved, q_list, q_count):
    highest = lax.Precision.HIGHEST
    band_width = 3 * ORB_DEV
    column_blocks = chibar.reshape(P_WIN, N_ATOM, QB_DEV * BLK)
    tensor_view = t_blocks.reshape(QL * BLK, N_TENS, N_ATOM, PAIR_DEV)
    saved_view = n_saved.reshape(P_WIN, N_ATOM, ORB_DEV, band_width)
    offsets = jnp.arange(-REACH, REACH + 1).astype(jnp.int32)

    def per_atom(atom_index):
        nearby = (atom_index + offsets) % N_ATOM
        neighbour = jnp.take(column_blocks, nearby.astype(jnp.int32), axis=1)
        neighbour = neighbour.reshape(P_WIN, (2 * REACH + 1) * QB_DEV, BLK)
        slot_ids = jnp.take(q_list, atom_index, axis=1)
        in_use = jnp.take(q_count, atom_index, axis=1)
        chosen = jnp.take(neighbour, slot_ids.astype(jnp.int32), axis=1)
        keeper = (jnp.arange(QL)[None, :] < in_use[:, None]).astype(jnp.float32)
        chosen = (chosen * keeper[None, :, :, None]).reshape(P_WIN, N_TENS, QL * BLK)
        tensor_part = jnp.take(tensor_view, atom_index, axis=2)
        mbar = jnp.einsum("ptk,ktc->tpc", chosen, tensor_part, precision=highest)
        mbar = mbar.reshape(N_TENS, P_WIN, NU_T, ORB_DEV)
        saved_part = jnp.take(saved_view, atom_index, axis=1)
        partial_value = jnp.einsum("tpjm,pml->tjl", mbar, saved_part, precision=highest)
        return partial_value.reshape(band_width, band_width)

    partials = lax.map(per_atom, jnp.arange(N_ATOM).astype(jnp.int32))
    blocks = partials.reshape(N_ATOM, 3, ORB_DEV, band_width)
    from_lower = jnp.roll(blocks[:, 2], 1, axis=0)
    from_upper = jnp.roll(blocks[:, 0], -1, axis=0)
    result = place_block(from_lower, 0, ORB_DEV) + place_block(blocks[:, 1], 1, ORB_DEV) + place_block(from_upper, 2, ORB_DEV)
    return result.reshape(NORB, 5 * ORB_DEV)
```

```python
from functools import partial

import jax
import jax.numpy as jnp
from jax import lax
from jax.experimental import pallas as pl
from jax.experimental.pallas import tpu as pltpu
from jax.sharding import PartitionSpec as P


LANES = 128
SUBL = 8
REACH = 3
VM = pl.BlockSpec(memory_space=pltpu.VMEM)
SM = pl.BlockSpec(memory_space=pltpu.SMEM)
HB = pl.BlockSpec(memory_space=pl.ANY)
f32 = jnp.float32
bf16 = jnp.bfloat16


def limit(mib):
    return pltpu.CompilerParams(vmem_limit_bytes=mib * 2**20)


def vmem(shape, dtype):
    return pltpu.VMEM(shape, dtype)


def split(x):
    hi = x.astype(bf16)
    return hi, (x - hi.astype(f32)).astype(bf16)


def shift(x, by):
    atoms = lax.axis_size("atom")
    return lax.ppermute(x, "atom", [(i, (i + by) % atoms) for i in range(atoms)])


def send(x, to):
    atoms = lax.axis_size("atom")
    pairs = []
    for t in range(2):
        for s in range(atoms):
            u, v = to(t, s)
            pairs.append((t * atoms + s, u * atoms + v % atoms))
    return lax.ppermute(x, ("tens", "atom"), pairs)


def prep_t(t_blocks):
    rows, cols = t_blocks.shape
    step = 64

    def body(src, hi, lo, buf, sems):
        copies = []
        for i in range(rows // step):
            here = pl.ds(i * step, step)
            copies.append(pltpu.make_async_copy(src.at[here], buf.at[here], sems.at[i]))
            copies[-1].start()
        for i in range(rows // step):
            copies[i].wait()

            def tile(c, carry, i=i):
                at = pl.ds(pl.multiple_of(c * 512, 512), 512)
                here = pl.ds(i * step, step)
                h, l = split(buf[here, at])
                hi[here, at] = h
                lo[here, at] = l
                return carry

            lax.fori_loop(0, cols // 512, tile, 0)

    return pl.pallas_call(
        body, in_specs=[HB], out_specs=[VM, VM],
        out_shape=[vmem((rows, cols), bf16), vmem((rows, cols), bf16)],
        scratch_shapes=[pltpu.VMEM((rows, cols), f32), pltpu.SemaphoreType.DMA((rows // step,))],
        name="prep_t", compiler_params=limit(14),
    )(t_blocks)


def prep_n(saved):
    def body(x, hi, lo):
        h, l = split(x[...])
        hi[...] = h
        lo[...] = l

    return pl.pallas_call(
        body, in_specs=[VM], out_specs=[VM, VM],
        out_shape=[vmem(saved.shape, bf16), vmem(saved.shape, bf16)], name="prep_n", compiler_params=limit(8),
    )(saved)


def select(pieces, q_list, q_count, p_rows, early):
    p_all, width = pieces[0].shape
    ql = q_list.shape[-1]
    blk = LANES
    qb = width // blk

    def body(*refs):
        parts, (ql_ref, qc_ref, out, scr) = refs[:len(pieces)], refs[len(pieces):]
        t = lax.axis_index("tens")
        for q in range(ql):
            want = ql_ref[0, 0, q]
            pick = parts[0][:, :blk]
            for i in range(1, len(parts) * qb):
                pick = jnp.where(want == i, parts[i // qb][:, (i % qb) * blk:(i % qb + 1) * blk], pick)
            scr[:, q * blk:(q + 1) * blk] = jnp.where(q < qc_ref[0, 0], pick, 0.0)
        other = (1 - t) * p_rows
        order = ((other + early, p_rows - early), (t * p_rows, p_rows), (other, early))
        at = 0
        for start, size in order:
            h, l = split(scr[pl.ds(pl.multiple_of(start, 16), size), :])
            out[at:at + size, :] = h
            out[p_all + at:p_all + at + size, :] = l
            at += size

    return pl.pallas_call(
        body, in_specs=[VM] * len(pieces) + [SM, SM], out_specs=VM,
        out_shape=vmem((2 * p_all, ql * blk), bf16),
        scratch_shapes=[pltpu.VMEM((p_all, ql * blk), f32)], name="select", compiler_params=limit(8),
    )(*pieces, q_list, q_count)


def multiply(chosen, t_hi, t_lo, first, cols, cross):
    p_all = chosen.shape[0] // 2
    own = p_all - cross
    ct = cols // LANES
    sub = 512 if cols % 512 == 0 else 256

    def body(c, hi, lo, out_c, out_o):
        for j in range(cols // sub):
            at = pl.ds(first + j * sub, sub)
            big = jnp.dot(c[...], hi[:, at], preferred_element_type=f32)
            val = big[:p_all] + big[p_all:] + jnp.dot(c[:p_all, :], lo[:, at], preferred_element_type=f32)
            for k in range(sub // LANES):
                jt = j * (sub // LANES) + k
                for i in range(p_all // SUBL):
                    v = val[i * SUBL:(i + 1) * SUBL, k * LANES:(k + 1) * LANES]
                    if i < cross // SUBL:
                        out_c[pl.ds((i * ct + jt) * SUBL, SUBL), :] = v
                    else:
                        out_o[pl.ds(((i - cross // SUBL) * ct + jt) * SUBL, SUBL), :] = v

    return pl.pallas_call(
        body, in_specs=[VM] * 3, out_specs=[VM, VM],
        out_shape=[vmem((cross * ct, LANES), f32), vmem((own * ct, LANES), f32)], name="multiply", compiler_params=limit(8),
    )(chosen, t_hi, t_lo)


def contract_into(x, rows, ct, n_parts, n_rows, l_hi, l_lo):
    lane = lax.broadcasted_iota(jnp.int32, (ct, LANES), 1)
    low = lane < LANES // 2
    for p in range(0, rows, 2):
        a, b = (x[pl.ds((q // SUBL) * ct * SUBL + q % SUBL, ct, stride=SUBL), :] for q in (p, p + 1))
        even = jnp.where(low, a, pltpu.roll(b, LANES // 2, 1))
        odd = jnp.where(low, pltpu.roll(a, LANES // 2, 1), b)
        at = pl.ds((p // 2) * LANES, LANES)
        for i, v in enumerate((even, odd)):
            h, l = split(v)
            l_hi[pl.ds(i * ct, ct), at] = h
            l_lo[pl.ds(i * ct, ct), at] = l
    half = LANES // 2
    total = None
    at = 0
    for (w_hi, w_lo), (start, count) in zip(n_parts, n_rows):
        k = pl.ds(at * half, count * half)
        w = pl.ds(start * half, count * half)
        v = jnp.dot(l_hi[:, k], w_hi[w, :], preferred_element_type=f32)
        v += jnp.dot(l_lo[:, k], w_hi[w, :], preferred_element_type=f32)
        v += jnp.dot(l_hi[:, k], w_lo[w, :], preferred_element_type=f32)
        total = v if total is None else total + v
        at += count
    return total


def store_rows(out, first, ct, val):
    band = val.shape[1]
    wide = jnp.concatenate([val, jnp.zeros((val.shape[0], out.shape[0] * LANES - band), f32)], axis=1)
    for i in range(2):
        for c in range(out.shape[0]):
            out[c, pl.ds(first + i, ct, stride=2), :] = wide[i * ct:(i + 1) * ct, c * LANES:(c + 1) * LANES]


def contract(stretches, firsts, rows, saved, n_rows, band, nu_t, orb, own, earlier=()):
    wide = -(-band // LANES)
    cts = [x.shape[0] // rows for x in stretches]
    last = own is not None
    flat = [w for pair in saved for w in pair]

    def body(*refs):
        refs = list(refs)
        xs = [refs.pop(0) for _ in stretches]
        ws = [refs.pop(0) for _ in flat]
        before = [refs.pop(0) for _ in earlier]
        outs = [refs.pop(0) for _ in range(2 if last else 1)]
        acc, scratch = (refs.pop(0), refs) if last else (outs[0], refs)
        pairs = list(zip(ws[0::2], ws[1::2]))
        base = 0
        for e, b in zip(earlier, before):
            acc[:, pl.ds(base, e.shape[1]), :] = b[...]
            base += e.shape[1]
        for i, (x, ct) in enumerate(zip(xs, cts)):
            val = contract_into(x, rows, ct, pairs, n_rows, scratch[2 * i], scratch[2 * i + 1])
            store_rows(acc, base, ct, val)
            base += 2 * ct
        if last:
            t = lax.axis_index("tens")
            u = t if own else 1 - t
            rest = nu_t - orb
            for out, start, size in ((outs[0], u * rest, orb), (outs[1], (1 - u) * orb, rest)):
                here = pl.ds(pl.multiple_of(start, SUBL), size)
                out[...] = jnp.concatenate([acc[c, here, :] for c in range(wide)], axis=1)[:, :band]

    if last:
        out_shape = [vmem((orb, band), f32), vmem((nu_t - orb, band), f32)]
        scratch = [pltpu.VMEM((wide, nu_t, LANES), f32)]
    else:
        out_shape = [vmem((wide, 2 * sum(cts), LANES), f32)]
        scratch = []
    for ct in cts:
        scratch += [pltpu.VMEM((2 * ct, rows * orb), bf16)] * 2
    return pl.pallas_call(
        body, in_specs=[VM] * (len(stretches) + len(flat) + len(earlier)), out_specs=[VM] * len(out_shape),
        out_shape=out_shape, scratch_shapes=scratch, name="contract", compiler_params=limit(12),
    )(*stretches, *flat, *earlier)


def finish(own, rec, orb, band):
    rest = own[0].shape[0]

    def body(ho, oa, ob, oc, hr, ra, rb, rc, out):
        t = lax.axis_index("tens")
        first = t == 0
        lower = jnp.where(first, ob[...], oa[...]) + jnp.where(first, ra[...], rb[...])
        upper = jnp.where(first, oa[...], ob[...]) + jnp.where(first, rb[...], ra[...])
        x = ho[...] + rc[...]
        y = oc[...] + hr[...]
        mid = jnp.concatenate([jnp.where(first, x, y), jnp.where(first, y, x)], axis=0)
        zero = jnp.zeros((orb, orb), f32)
        out[...] = (jnp.concatenate([lower, zero, zero], axis=1) + jnp.concatenate([zero, mid, zero], axis=1)
                    + jnp.concatenate([zero, zero, upper], axis=1))

    return pl.pallas_call(
        body, in_specs=[VM] * 8, out_specs=VM,
        out_shape=jax.ShapeDtypeStruct((orb, band + 2 * orb), f32), name="finish", compiler_params=limit(8),
    )(*own, *rec)


def paired(chibar, t_blocks, n_saved, q_list, q_count):
    p_rows, n_cols = n_saved.shape
    orb = LANES // 2
    band = n_cols // orb
    cols = t_blocks.shape[1]
    nu_t = cols // orb
    early = 16
    cross = p_rows - early
    swap = [(0, 1), (1, 0)]

    n_far = lax.ppermute(n_saved[:early], "tens", swap)
    pieces = [chibar if o == 0 else shift(chibar, -o) for o in range(-REACH, REACH + 1)]
    t_hi, t_lo = prep_t(t_blocks)
    chosen = select(pieces, q_list, q_count, p_rows, early)

    widths = [cols // 3] * 3
    mine, far = [], []
    first = 0
    for w in widths:
        c, o = multiply(chosen, t_hi, t_lo, first, w, cross)
        far.append(lax.ppermute(c, "tens", swap))
        mine.append(o)
        first += w

    near = prep_n(n_saved.reshape(p_rows * orb, band))
    beyond = prep_n(n_far.reshape(early * orb, band))
    main, rest = contract(mine, None, p_rows + early, [near, beyond], [(0, p_rows), (0, early)], band, nu_t, orb, True)
    oa = send(main, lambda t, s: (t, s - 1 + 2 * t))
    ob = send(main, lambda t, s: (1 - t, s - 1 + 2 * t))
    oc = send(rest, lambda t, s: (1 - t, s))
    done = []
    for x in far[:-1]:
        done += contract([x], None, cross, [near], [(early, cross)], band, nu_t, orb, None)
    r_main, r_rest = contract(far[-1:], None, cross, [near], [(early, cross)], band, nu_t, orb, False, done)
    ra = send(r_main, lambda t, s: (t, s + 1 - 2 * t))
    rb = send(r_main, lambda t, s: (1 - t, s + 1 - 2 * t))
    rc = send(r_rest, lambda t, s: (1 - t, s))
    return finish((rest, oa, ob, oc), (r_rest, ra, rb, rc), orb, band)


def general(chibar, t_blocks, n_saved, q_list, q_count):
    tens = lax.axis_size("tens")
    t = lax.axis_index("tens")
    p_rows, n_cols = n_saved.shape
    blk = t_blocks.shape[0] // q_list.shape[-1]
    ql = q_list.shape[-1]
    qb = chibar.shape[1] // blk
    reach = REACH
    orb = int(round((n_cols // 3) ** 0.5))
    band = 3 * orb
    nu_t = t_blocks.shape[1] // orb
    high = lax.Precision.HIGH
    slot_ids = q_list.reshape(ql)
    in_use = q_count.reshape(())
    keeper = jnp.arange(ql) < in_use

    def chosen_of(r):
        rows = lax.dynamic_slice_in_dim(chibar, ((t + r) % tens) * p_rows, p_rows, 0)
        pieces = [rows if o == 0 else shift(rows, -o) for o in range(-reach, reach + 1)]
        blocks = [pc[:, b * blk:(b + 1) * blk] for pc in pieces for b in range(qb)]
        out = []
        for q in range(ql):
            pick = blocks[0]
            for i in range(1, len(blocks)):
                pick = jnp.where(slot_ids[q] == i, blocks[i], pick)
            out.append(jnp.where(keeper[q], pick, 0.0))
        return jnp.concatenate(out, axis=1)

    saved = n_saved.reshape(p_rows, orb, band)
    parts = []
    mb = []
    for r in list(range(1, tens)) + [0]:
        m = jnp.dot(chosen_of(r), t_blocks, precision=high, preferred_element_type=jnp.float32)
        if r:
            m = lax.ppermute(m, "tens", [(i, (i + r) % tens) for i in range(tens)])
        mb.append(m)
    mb = [mb[-1]] + mb[:-1]
    for r in range(tens):
        parts.append(jnp.einsum("pnm,pml->nl", mb[r].reshape(p_rows, nu_t, orb), saved, precision=high,
                                preferred_element_type=jnp.float32))
    stacked = jnp.stack(parts)
    order = (t - jnp.arange(tens)) % tens
    if tens == 2:
        partial = jnp.where(t == 0, stacked, stacked[::-1]).reshape(band, band)
    else:
        partial = jnp.take(stacked, order, axis=0).reshape(band, band)
    blocks = partial.reshape(3, orb, band)
    lower = shift(blocks[2], 1)
    upper = shift(blocks[0], -1)
    pad = lambda x, o: jnp.pad(x, ((0, 0), (o * orb, (2 - o) * orb)))
    res = pad(lower, 0) + pad(blocks[1], 1) + pad(upper, 2)
    if tens == 2:
        return res + lax.ppermute(res, "tens", [(0, 1), (1, 0)])
    return lax.psum(res, "tens")


def solution(mesh):
    placed = (
        P(None, "atom"),
        P(None, ("tens", "atom")),
        P("tens", "atom"),
        P("tens", "atom", None),
        P("tens", "atom"),
    )
    body = paired if mesh.shape["tens"] == 2 else general
    return jax.shard_map(body, mesh=mesh, in_specs=placed, out_specs=P("atom", None), check_vma=False)
```

```python
from functools import partial

import jax
import jax.numpy as jnp
from jax import lax
from jax.experimental import pallas as pl
from jax.experimental.pallas import tpu as pltpu
from jax.sharding import PartitionSpec as P


LANES = 128
SUBL = 8
REACH = 3
VM = pl.BlockSpec(memory_space=pltpu.VMEM)
SM = pl.BlockSpec(memory_space=pltpu.SMEM)
HB = pl.BlockSpec(memory_space=pltpu.HBM)
f32 = jnp.float32
bf16 = jnp.bfloat16


def limit(mib):
    return pltpu.CompilerParams(vmem_limit_bytes=mib * 2**20)


def vmem(shape, dtype):
    return pltpu.VMEM(shape, dtype)


def split(x):
    hi = x.astype(bf16)
    return hi, (x - hi.astype(f32)).astype(bf16)


def shift(x, by):
    atoms = lax.axis_size("atom")
    return lax.ppermute(x, "atom", [(i, (i + by) % atoms) for i in range(atoms)])


def send(x, to):
    atoms = lax.axis_size("atom")
    pairs = []
    for t in range(2):
        for s in range(atoms):
            u, v = to(t, s)
            pairs.append((t * atoms + s, u * atoms + v % atoms))
    return lax.ppermute(x, ("tens", "atom"), pairs)


def prep_t(t_blocks):
    rows, cols = t_blocks.shape
    step = 64

    def body(src, hi, lo, buf, sems):
        copies = []
        for i in range(rows // step):
            here = pl.ds(i * step, step)
            copies.append(pltpu.make_async_copy(src.at[here], buf.at[here], sems.at[i]))
            copies[-1].start()
        for i in range(rows // step):
            copies[i].wait()

            def tile(c, carry, i=i):
                at = pl.ds(pl.multiple_of(c * 512, 512), 512)
                here = pl.ds(i * step, step)
                h, l = split(buf[here, at])
                hi[here, at] = h
                lo[here, at] = l
                return carry

            lax.fori_loop(0, cols // 512, tile, 0)

    return pl.pallas_call(
        body, in_specs=[HB], out_specs=[VM, VM],
        out_shape=[vmem((rows, cols), bf16), vmem((rows, cols), bf16)],
        scratch_shapes=[pltpu.VMEM((rows, cols), f32), pltpu.SemaphoreType.DMA((rows // step,))],
        name="prep_t", compiler_params=limit(14),
    )(t_blocks)


def head(x, rows):
    def body(src, out, sem):
        copy = pltpu.make_async_copy(src.at[pl.ds(0, rows)], out, sem)
        copy.start()
        copy.wait()

    return pl.pallas_call(
        body, in_specs=[HB], out_specs=VM, out_shape=vmem((rows, x.shape[1]), x.dtype),
        scratch_shapes=[pltpu.SemaphoreType.DMA], name="head", compiler_params=limit(4),
    )(x)


def prep_n(saved, orb, band):
    rows, cols = saved.shape
    groups = rows // SUBL
    half = LANES // 2
    pairs = orb // 2
    wide = 2 * LANES

    def body(src, hi, lo, buf, tiles, tmp, sems):
        def copy(i):
            here = pl.ds(pl.multiple_of(i * SUBL, SUBL), SUBL)
            return pltpu.make_async_copy(src.at[here], buf.at[here], sems.at[i])

        for i in range(groups):
            copy(i).start()
        low = lax.broadcasted_iota(jnp.int32, (pairs, LANES), 1) < half

        def group(i, carry):
            copy(i).wait()
            here = pl.ds(pl.multiple_of(i * SUBL, SUBL), SUBL)
            for c in range(cols // LANES):
                tiles[c * SUBL:(c + 1) * SUBL, :] = buf[here, c * LANES:(c + 1) * LANES]
            for r in range(SUBL):
                v = [tiles[pl.ds(k * SUBL + r, pairs, stride=3 * SUBL), :] for k in range(3)]
                w1, w2 = (pltpu.roll(x, half, 1) for x in v[1:])
                tmp[r, 0, pl.ds(0, pairs, stride=2), :] = v[0]
                tmp[r, 1, pl.ds(0, pairs, stride=2), :] = v[1]
                tmp[r, 0, pl.ds(1, pairs, stride=2), :] = jnp.where(low, w1, w2)
                tmp[r, 1, pl.ds(1, pairs, stride=2), :] = w2
                at = pl.ds(pl.multiple_of(i * SUBL * orb + r * orb, orb), orb)
                for k in range(2):
                    h, l = split(tmp[r, k])
                    hi[at, k * LANES:(k + 1) * LANES] = h
                    lo[at, k * LANES:(k + 1) * LANES] = l
            return carry

        lax.fori_loop(0, groups, group, 0)

    return pl.pallas_call(
        body, in_specs=[HB], out_specs=[VM, VM],
        out_shape=[vmem((rows * orb, wide), bf16)] * 2,
        scratch_shapes=[pltpu.VMEM((rows, cols), f32), pltpu.VMEM((cols // LANES * SUBL, LANES), f32),
                        pltpu.VMEM((SUBL, 2, orb, LANES), f32), pltpu.SemaphoreType.DMA((groups,))],
        name="prep_n", compiler_params=limit(10),
    )(saved)


def select(pieces, q_list, q_count, p_rows, early, after):
    p_all, width = pieces[0].shape
    ql = q_list.shape[-1]
    blk = LANES
    qb = width // blk

    def body(*refs):
        parts, (ql_ref, qc_ref, _, out, scr) = refs[:len(pieces)], refs[len(pieces):]
        t = lax.axis_index("tens")
        for q in range(ql):
            want = ql_ref[0, 0, q]
            pick = parts[0][:, :blk]
            for i in range(1, len(parts) * qb):
                pick = jnp.where(want == i, parts[i // qb][:, (i % qb) * blk:(i % qb + 1) * blk], pick)
            scr[:, q * blk:(q + 1) * blk] = jnp.where(q < qc_ref[0, 0], pick, 0.0)
        other = (1 - t) * p_rows
        order = ((other + early, p_rows - early), (t * p_rows, p_rows), (other, early))
        at = 0
        for start, size in order:
            h, l = split(scr[pl.ds(pl.multiple_of(start, 16), size), :])
            out[at:at + size, :] = h
            out[p_all + at:p_all + at + size, :] = l
            at += size

    return pl.pallas_call(
        body, in_specs=[VM] * len(pieces) + [SM, SM, VM], out_specs=VM,
        out_shape=vmem((2 * p_all, ql * blk), bf16),
        scratch_shapes=[pltpu.VMEM((p_all, ql * blk), f32)], name="select", compiler_params=limit(8),
    )(*pieces, q_list, q_count, after)


def multiply(chosen, t_hi, t_lo, first, cols, cross):
    p_all = chosen.shape[0] // 2
    own = p_all - cross
    ct = cols // LANES
    sub = 512 if cols % 512 == 0 else 256

    def body(c, hi, lo, out_c, out_o):
        for j in range(cols // sub):
            at = pl.ds(first + j * sub, sub)
            big = jnp.dot(c[...], hi[:, at], preferred_element_type=f32)
            val = big[:p_all] + big[p_all:] + jnp.dot(c[:p_all, :], lo[:, at], preferred_element_type=f32)
            for k in range(sub // LANES):
                jt = j * (sub // LANES) + k
                for i in range(p_all // SUBL):
                    v = val[i * SUBL:(i + 1) * SUBL, k * LANES:(k + 1) * LANES]
                    if i < cross // SUBL:
                        out_c[pl.ds((i * ct + jt) * SUBL, SUBL), :] = v
                    else:
                        out_o[pl.ds(((i - cross // SUBL) * ct + jt) * SUBL, SUBL), :] = v

    return pl.pallas_call(
        body, in_specs=[VM] * 3, out_specs=[VM, VM],
        out_shape=[vmem((cross * ct, LANES), f32), vmem((own * ct, LANES), f32)], name="multiply", compiler_params=limit(8),
    )(chosen, t_hi, t_lo)


def contract_into(x, rows, ct, n_parts, n_rows, l_hi, l_lo):
    lane = lax.broadcasted_iota(jnp.int32, (ct, LANES), 1)
    low = lane < LANES // 2
    for p in range(0, rows, 2):
        a, b = (x[pl.ds((q // SUBL) * ct * SUBL + q % SUBL, ct, stride=SUBL), :] for q in (p, p + 1))
        even = jnp.where(low, a, pltpu.roll(b, LANES // 2, 1))
        odd = jnp.where(low, pltpu.roll(a, LANES // 2, 1), b)
        at = pl.ds((p // 2) * LANES, LANES)
        for i, v in enumerate((even, odd)):
            h, l = split(v)
            l_hi[pl.ds(i * ct, ct), at] = h
            l_lo[pl.ds(i * ct, ct), at] = l
    half = LANES // 2
    total = None
    at = 0
    for (w_hi, w_lo), (start, count) in zip(n_parts, n_rows):
        k = pl.ds(at * half, count * half)
        w = pl.ds(start * half, count * half)
        v = jnp.dot(l_hi[:, k], w_hi[w, :], preferred_element_type=f32)
        v += jnp.dot(l_lo[:, k], w_hi[w, :], preferred_element_type=f32)
        v += jnp.dot(l_hi[:, k], w_lo[w, :], preferred_element_type=f32)
        total = v if total is None else total + v
        at += count
    return total


def store_rows(out, first, ct, val):
    band = val.shape[1]
    wide = jnp.concatenate([val, jnp.zeros((val.shape[0], out.shape[0] * LANES - band), f32)], axis=1)
    for i in range(2):
        for c in range(out.shape[0]):
            out[c, pl.ds(first + i, ct, stride=2), :] = wide[i * ct:(i + 1) * ct, c * LANES:(c + 1) * LANES]


def contract(stretches, rows, saved, n_rows, band, nu_t, orb, own, earlier=(), after=()):
    wide = -(-band // LANES)
    cts = [x.shape[0] // rows for x in stretches]
    last = own is not None
    flat = [w for pair in saved for w in pair]

    def body(*refs):
        refs = list(refs)
        xs = [refs.pop(0) for _ in stretches]
        ws = [refs.pop(0) for _ in flat]
        before = [refs.pop(0) for _ in earlier]
        del refs[:len(after)]
        outs = [refs.pop(0) for _ in range(2 if last else 1)]
        acc, scratch = (refs.pop(0), refs) if last else (outs[0], refs)
        pairs = list(zip(ws[0::2], ws[1::2]))
        base = 0
        for e, b in zip(earlier, before):
            acc[:, pl.ds(base, e.shape[1]), :] = b[...]
            base += e.shape[1]
        for i, (x, ct) in enumerate(zip(xs, cts)):
            val = contract_into(x, rows, ct, pairs, n_rows, scratch[2 * i], scratch[2 * i + 1])[:, :band]
            store_rows(acc, base, ct, val)
            base += 2 * ct
        if last:
            t = lax.axis_index("tens")
            u = t if own else 1 - t
            rest = nu_t - orb
            for out, start, size in ((outs[0], u * rest, orb), (outs[1], (1 - u) * orb, rest)):
                here = pl.ds(pl.multiple_of(start, SUBL), size)
                out[...] = jnp.concatenate([acc[c, here, :] for c in range(wide)], axis=1)[:, :band]

    if last:
        out_shape = [vmem((orb, band), f32), vmem((nu_t - orb, band), f32)]
        scratch = [pltpu.VMEM((wide, nu_t, LANES), f32)]
    else:
        out_shape = [vmem((wide, 2 * sum(cts), LANES), f32)]
        scratch = []
    for ct in cts:
        scratch += [pltpu.VMEM((2 * ct, rows * orb), bf16)] * 2
    return pl.pallas_call(
        body, in_specs=[VM] * (len(stretches) + len(flat) + len(earlier) + len(after)), out_specs=[VM] * len(out_shape),
        out_shape=out_shape, scratch_shapes=scratch, name="contract", compiler_params=limit(12),
    )(*stretches, *flat, *earlier, *after)


def finish(own, rec, orb, band):
    rest = own[0].shape[0]

    def body(ho, oa, ob, oc, hr, ra, rb, rc, out):
        t = lax.axis_index("tens")
        first = t == 0
        lower = jnp.where(first, ob[...], oa[...]) + jnp.where(first, ra[...], rb[...])
        upper = jnp.where(first, oa[...], ob[...]) + jnp.where(first, rb[...], ra[...])
        x = ho[...] + rc[...]
        y = oc[...] + hr[...]
        mid = jnp.concatenate([jnp.where(first, x, y), jnp.where(first, y, x)], axis=0)
        zero = jnp.zeros((orb, orb), f32)
        out[...] = (jnp.concatenate([lower, zero, zero], axis=1) + jnp.concatenate([zero, mid, zero], axis=1)
                    + jnp.concatenate([zero, zero, upper], axis=1))

    return pl.pallas_call(
        body, in_specs=[VM] * 8, out_specs=VM,
        out_shape=jax.ShapeDtypeStruct((orb, band + 2 * orb), f32), name="finish", compiler_params=limit(8),
    )(*own, *rec)


def paired(chibar, t_blocks, n_saved, q_list, q_count):
    p_rows, n_cols = n_saved.shape
    orb = LANES // 2
    band = n_cols // orb
    cols = t_blocks.shape[1]
    nu_t = cols // orb
    early = 16
    cross = p_rows - early
    swap = [(0, 1), (1, 0)]

    n_saved = pltpu.with_memory_space_constraint(n_saved, pltpu.HBM)
    t_blocks = pltpu.with_memory_space_constraint(t_blocks, pltpu.HBM)
    n_far = lax.ppermute(head(n_saved, early), "tens", swap)
    pieces = [chibar if o == 0 else shift(chibar, -o) for o in range(-REACH, REACH + 1)]
    t_hi, t_lo = prep_t(t_blocks)
    near = prep_n(n_saved, orb, band)
    chosen = select(pieces, q_list, q_count, p_rows, early, near[0])

    widths = [cols // 3] * 3
    mine, far = [], []
    first = 0
    for w in widths:
        c, o = multiply(chosen, t_hi, t_lo, first, w, cross)
        far.append(lax.ppermute(c, "tens", swap))
        mine.append(o)
        first += w

    beyond = prep_n(n_far, orb, band)
    main, rest = contract(mine, p_rows + early, [near, beyond], [(0, p_rows), (0, early)], band, nu_t, orb, True)
    oa = send(main, lambda t, s: (t, s - 1 + 2 * t))
    ob = send(main, lambda t, s: (1 - t, s - 1 + 2 * t))
    oc = send(rest, lambda t, s: (1 - t, s))
    done = []
    for x in far[:-1]:
        done += contract([x], cross, [near], [(early, cross)], band, nu_t, orb, None, after=(main,))
    r_main, r_rest = contract(far[-1:], cross, [near], [(early, cross)], band, nu_t, orb, False, done,
                            after=(oa, ob, oc))
    ra = send(r_main, lambda t, s: (t, s + 1 - 2 * t))
    rb = send(r_main, lambda t, s: (1 - t, s + 1 - 2 * t))
    rc = send(r_rest, lambda t, s: (1 - t, s))
    return finish((rest, oa, ob, oc), (r_rest, ra, rb, rc), orb, band)


def general(chibar, t_blocks, n_saved, q_list, q_count):
    tens = lax.axis_size("tens")
    t = lax.axis_index("tens")
    p_rows, n_cols = n_saved.shape
    blk = t_blocks.shape[0] // q_list.shape[-1]
    ql = q_list.shape[-1]
    qb = chibar.shape[1] // blk
    reach = REACH
    orb = int(round((n_cols // 3) ** 0.5))
    band = 3 * orb
    nu_t = t_blocks.shape[1] // orb
    high = lax.Precision.HIGH
    slot_ids = q_list.reshape(ql)
    in_use = q_count.reshape(())
    keeper = jnp.arange(ql) < in_use

    def chosen_of(r):
        rows = lax.dynamic_slice_in_dim(chibar, ((t + r) % tens) * p_rows, p_rows, 0)
        pieces = [rows if o == 0 else shift(rows, -o) for o in range(-reach, reach + 1)]
        blocks = [pc[:, b * blk:(b + 1) * blk] for pc in pieces for b in range(qb)]
        out = []
        for q in range(ql):
            pick = blocks[0]
            for i in range(1, len(blocks)):
                pick = jnp.where(slot_ids[q] == i, blocks[i], pick)
            out.append(jnp.where(keeper[q], pick, 0.0))
        return jnp.concatenate(out, axis=1)

    saved = n_saved.reshape(p_rows, orb, band)
    parts = []
    mb = []
    for r in list(range(1, tens)) + [0]:
        m = jnp.dot(chosen_of(r), t_blocks, precision=high, preferred_element_type=jnp.float32)
        if r:
            m = lax.ppermute(m, "tens", [(i, (i + r) % tens) for i in range(tens)])
        mb.append(m)
    mb = [mb[-1]] + mb[:-1]
    for r in range(tens):
        parts.append(jnp.einsum("pnm,pml->nl", mb[r].reshape(p_rows, nu_t, orb), saved, precision=high,
                                preferred_element_type=jnp.float32))
    stacked = jnp.stack(parts)
    order = (t - jnp.arange(tens)) % tens
    if tens == 2:
        partial = jnp.where(t == 0, stacked, stacked[::-1]).reshape(band, band)
    else:
        partial = jnp.take(stacked, order, axis=0).reshape(band, band)
    blocks = partial.reshape(3, orb, band)
    lower = shift(blocks[2], 1)
    upper = shift(blocks[0], -1)
    pad = lambda x, o: jnp.pad(x, ((0, 0), (o * orb, (2 - o) * orb)))
    res = pad(lower, 0) + pad(blocks[1], 1) + pad(upper, 2)
    if tens == 2:
        return res + lax.ppermute(res, "tens", [(0, 1), (1, 0)])
    return lax.psum(res, "tens")


def solution(mesh):
    placed = (
        P(None, "atom"),
        P(None, ("tens", "atom")),
        P("tens", "atom"),
        P("tens", "atom", None),
        P("tens", "atom"),
    )
    body = paired if mesh.shape["tens"] == 2 else general
    return jax.shard_map(body, mesh=mesh, in_specs=placed, out_specs=P("atom", None), check_vma=False)
```

```python
import jax
import jax.numpy as jnp
from jax import lax
from jax.experimental import pallas as pl
from jax.experimental.pallas import tpu as pltpu
from jax.sharding import PartitionSpec as P


LANES = 128
SUBL = 8
REACH = 3
VM = pl.BlockSpec(memory_space=pltpu.VMEM)
SM = pl.BlockSpec(memory_space=pltpu.SMEM)
HB = pl.BlockSpec(memory_space=pltpu.HBM)
f32 = jnp.float32
bf16 = jnp.bfloat16


def limit(mib):
    return pltpu.CompilerParams(vmem_limit_bytes=mib * 2**20)


def vmem(shape, dtype):
    return pltpu.VMEM(shape, dtype)


def split(x):
    hi = x.astype(bf16)
    return hi, (x - hi.astype(f32)).astype(bf16)


def shift(x, by):
    atoms = lax.axis_size("atom")
    return lax.ppermute(x, "atom", [(i, (i + by) % atoms) for i in range(atoms)])


def send(x, to):
    atoms = lax.axis_size("atom")
    pairs = []
    for t in range(2):
        for s in range(atoms):
            u, v = to(t, s)
            pairs.append((t * atoms + s, u * atoms + v % atoms))
    return lax.ppermute(x, ("tens", "atom"), pairs)


def prep_t(t_blocks):
    rows, cols = t_blocks.shape
    step = 64

    def body(src, hi, lo, buf, sems):
        copies = []
        for i in range(rows // step):
            here = pl.ds(i * step, step)
            copies.append(pltpu.make_async_copy(src.at[here], buf.at[here], sems.at[i]))
            copies[-1].start()
        for i in range(rows // step):
            copies[i].wait()

            def tile(c, carry, i=i):
                at = pl.ds(pl.multiple_of(c * 512, 512), 512)
                here = pl.ds(i * step, step)
                h, l = split(buf[here, at])
                hi[here, at] = h
                lo[here, at] = l
                return carry

            lax.fori_loop(0, cols // 512, tile, 0)

    return pl.pallas_call(
        body, in_specs=[HB], out_specs=[VM, VM],
        out_shape=[vmem((rows, cols), bf16), vmem((rows, cols), bf16)],
        scratch_shapes=[pltpu.VMEM((rows, cols), f32), pltpu.SemaphoreType.DMA((rows // step,))],
        name="prep_t", compiler_params=limit(14),
    )(t_blocks)


def head(x, rows):
    def body(src, out, sem):
        copy = pltpu.make_async_copy(src.at[pl.ds(0, rows)], out, sem)
        copy.start()
        copy.wait()

    return pl.pallas_call(
        body, in_specs=[HB], out_specs=VM, out_shape=vmem((rows, x.shape[1]), x.dtype),
        scratch_shapes=[pltpu.SemaphoreType.DMA], name="head", compiler_params=limit(4),
    )(x)


def prep_n(saved, orb):
    rows, cols = saved.shape
    groups = rows // SUBL
    half = LANES // 2
    pairs = orb // 2
    wide = 2 * LANES

    def body(src, hi, lo, buf, tiles, tmp, sems):
        def copy(i):
            here = pl.ds(pl.multiple_of(i * SUBL, SUBL), SUBL)
            return pltpu.make_async_copy(src.at[here], buf.at[here], sems.at[i])

        for i in range(groups):
            copy(i).start()
        low = lax.broadcasted_iota(jnp.int32, (pairs, LANES), 1) < half

        def group(i, carry):
            copy(i).wait()
            here = pl.ds(pl.multiple_of(i * SUBL, SUBL), SUBL)
            for c in range(cols // LANES):
                tiles[c * SUBL:(c + 1) * SUBL, :] = buf[here, c * LANES:(c + 1) * LANES]
            for r in range(SUBL):
                v = [tiles[pl.ds(k * SUBL + r, pairs, stride=3 * SUBL), :] for k in range(3)]
                w1, w2 = (pltpu.roll(x, half, 1) for x in v[1:])
                tmp[r, 0, pl.ds(0, pairs, stride=2), :] = v[0]
                tmp[r, 1, pl.ds(0, pairs, stride=2), :] = v[1]
                tmp[r, 0, pl.ds(1, pairs, stride=2), :] = jnp.where(low, w1, w2)
                tmp[r, 1, pl.ds(1, pairs, stride=2), :] = w2
                at = pl.ds(pl.multiple_of(i * SUBL * orb + r * orb, orb), orb)
                for k in range(2):
                    h, l = split(tmp[r, k])
                    hi[at, k * LANES:(k + 1) * LANES] = h
                    lo[at, k * LANES:(k + 1) * LANES] = l
            return carry

        lax.fori_loop(0, groups, group, 0)

    return pl.pallas_call(
        body, in_specs=[HB], out_specs=[VM, VM],
        out_shape=[vmem((rows * orb, wide), bf16)] * 2,
        scratch_shapes=[pltpu.VMEM((rows, cols), f32), pltpu.VMEM((cols // LANES * SUBL, LANES), f32),
                        pltpu.VMEM((SUBL, 2, orb, LANES), f32), pltpu.SemaphoreType.DMA((groups,))],
        name="prep_n", compiler_params=limit(10),
    )(saved)


def select(pieces, q_list, q_count, p_rows, early, after):
    p_all, width = pieces[0].shape
    ql = q_list.shape[-1]
    blk = LANES
    qb = width // blk

    def body(*refs):
        parts, (ql_ref, qc_ref, _, out, scr) = refs[:len(pieces)], refs[len(pieces):]
        t = lax.axis_index("tens")
        for q in range(ql):
            want = ql_ref[0, 0, q]
            pick = parts[0][:, :blk]
            for i in range(1, len(parts) * qb):
                pick = jnp.where(want == i, parts[i // qb][:, (i % qb) * blk:(i % qb + 1) * blk], pick)
            scr[:, q * blk:(q + 1) * blk] = jnp.where(q < qc_ref[0, 0], pick, 0.0)
        other = (1 - t) * p_rows
        order = ((other + early, p_rows - early), (t * p_rows, p_rows), (other, early))
        at = 0
        for start, size in order:
            h, l = split(scr[pl.ds(pl.multiple_of(start, 16), size), :])
            out[at:at + size, :] = h
            out[p_all + at:p_all + at + size, :] = l
            at += size

    return pl.pallas_call(
        body, in_specs=[VM] * len(pieces) + [SM, SM, VM], out_specs=VM,
        out_shape=vmem((2 * p_all, ql * blk), bf16),
        scratch_shapes=[pltpu.VMEM((p_all, ql * blk), f32)], name="select", compiler_params=limit(8),
    )(*pieces, q_list, q_count, after)


def multiply(chosen, t_hi, t_lo, first, slope, cols, cross):
    p_all = chosen.shape[0] // 2
    own = p_all - cross
    ct = cols // LANES
    sub = 512 if cols % 512 == 0 else 256

    def body(c, hi, lo, out_c, out_o):
        start = first + slope * lax.axis_index("tens")
        for j in range(cols // sub):
            at = pl.ds(pl.multiple_of(start + j * sub, LANES), sub)
            big = jnp.dot(c[...], hi[:, at], preferred_element_type=f32)
            val = big[:p_all] + big[p_all:] + jnp.dot(c[:p_all, :], lo[:, at], preferred_element_type=f32)
            for k in range(sub // LANES):
                jt = j * (sub // LANES) + k
                for i in range(p_all // SUBL):
                    v = val[i * SUBL:(i + 1) * SUBL, k * LANES:(k + 1) * LANES]
                    if i < cross // SUBL:
                        out_c[pl.ds((i * ct + jt) * SUBL, SUBL), :] = v
                    else:
                        out_o[pl.ds(((i - cross // SUBL) * ct + jt) * SUBL, SUBL), :] = v

    return pl.pallas_call(
        body, in_specs=[VM] * 3, out_specs=[VM, VM],
        out_shape=[vmem((cross * ct, LANES), f32), vmem((own * ct, LANES), f32)], name="multiply", compiler_params=limit(8),
    )(chosen, t_hi, t_lo)


def contract_into(x, rows, ct, n_parts, n_rows, l_hi, l_lo):
    lane = lax.broadcasted_iota(jnp.int32, (ct, LANES), 1)
    low = lane < LANES // 2
    for p in range(0, rows, 2):
        a, b = (x[pl.ds((q // SUBL) * ct * SUBL + q % SUBL, ct, stride=SUBL), :] for q in (p, p + 1))
        even = jnp.where(low, a, pltpu.roll(b, LANES // 2, 1))
        odd = jnp.where(low, pltpu.roll(a, LANES // 2, 1), b)
        at = pl.ds((p // 2) * LANES, LANES)
        for i, v in enumerate((even, odd)):
            h, l = split(v)
            l_hi[pl.ds(i * ct, ct), at] = h
            l_lo[pl.ds(i * ct, ct), at] = l
    half = LANES // 2
    total = None
    at = 0
    for (w_hi, w_lo), (start, count) in zip(n_parts, n_rows):
        k = pl.ds(at * half, count * half)
        w = pl.ds(start * half, count * half)
        v = jnp.dot(l_hi[:, k], w_hi[w, :], preferred_element_type=f32)
        v += jnp.dot(l_lo[:, k], w_hi[w, :], preferred_element_type=f32)
        v += jnp.dot(l_hi[:, k], w_lo[w, :], preferred_element_type=f32)
        total = v if total is None else total + v
        at += count
    return total


def contract(stretches, rows, saved, n_rows, band, sizes, after=()):
    wide = -(-band // LANES)
    cts = [x.shape[0] // rows for x in stretches]
    flat = [w for pair in saved for w in pair]

    def body(*refs):
        refs = list(refs)
        xs = [refs.pop(0) for _ in stretches]
        ws = [refs.pop(0) for _ in flat]
        del refs[:len(after)]
        outs = [refs.pop(0) for _ in sizes]
        acc = refs.pop(0)
        pairs = list(zip(ws[0::2], ws[1::2]))
        base = 0
        for i, (x, ct) in enumerate(zip(xs, cts)):
            val = contract_into(x, rows, ct, pairs, n_rows, refs[2 * i], refs[2 * i + 1])
            for par in range(2):
                for c in range(wide):
                    acc[c, pl.ds(base + par, ct, stride=2), :] = val[par * ct:(par + 1) * ct, c * LANES:(c + 1) * LANES]
            base += 2 * ct
        at = 0
        for out, size in zip(outs, sizes):
            out[...] = jnp.concatenate([acc[c, at:at + size, :] for c in range(wide)], axis=1)[:, :band]
            at += size

    scratch = [pltpu.VMEM((wide, 2 * sum(cts), LANES), f32)]
    for x, ct in zip(stretches, cts):
        scratch += [pltpu.VMEM((2 * ct, rows * LANES // 2), bf16)] * 2
    return pl.pallas_call(
        body, in_specs=[VM] * (len(stretches) + len(flat) + len(after)), out_specs=[VM] * len(sizes),
        out_shape=[vmem((size, band), f32) for size in sizes], scratch_shapes=scratch,
        name="contract", compiler_params=limit(12),
    )(*stretches, *flat, *after)


def finish(own, rec, orb, band):
    def body(ho, oa, ob, oc, hr, ra, rb, rc, out):
        t = lax.axis_index("tens")
        first = t == 0
        lower = jnp.where(first, ob[...], oa[...]) + jnp.where(first, ra[...], rb[...])
        upper = jnp.where(first, oa[...], ob[...]) + jnp.where(first, rb[...], ra[...])
        x = ho[...] + rc[...]
        y = oc[...] + hr[...]
        mid = jnp.concatenate([jnp.where(first, x, y), jnp.where(first, y, x)], axis=0)
        zero = jnp.zeros((orb, orb), f32)
        out[...] = (jnp.concatenate([lower, zero, zero], axis=1) + jnp.concatenate([zero, mid, zero], axis=1)
                    + jnp.concatenate([zero, zero, upper], axis=1))

    return pl.pallas_call(
        body, in_specs=[VM] * 8, out_specs=VM,
        out_shape=jax.ShapeDtypeStruct((orb, band + 2 * orb), f32), name="finish", compiler_params=limit(8),
    )(*own, *rec)


def paired(chibar, t_blocks, n_saved, q_list, q_count):
    p_rows, n_cols = n_saved.shape
    orb = LANES // 2
    band = n_cols // orb
    nu_t = t_blocks.shape[1] // orb
    early = 16
    cross = p_rows - early
    swap = [(0, 1), (1, 0)]

    n_saved = pltpu.with_memory_space_constraint(n_saved, pltpu.HBM)
    t_blocks = pltpu.with_memory_space_constraint(t_blocks, pltpu.HBM)
    n_far = lax.ppermute(head(n_saved, early), "tens", swap)
    pieces = [chibar if o == 0 else shift(chibar, -o) for o in range(-REACH, REACH + 1)]
    t_hi, t_lo = prep_t(t_blocks)
    near = prep_n(n_saved, orb)
    chosen = select(pieces, q_list, q_count, p_rows, early, near[0])

    rest = nu_t - orb
    far_main, own_main = multiply(chosen, t_hi, t_lo, 0, rest * orb, orb * orb, cross)
    far_main = lax.ppermute(far_main, "tens", swap)
    far_rest, own_rest = multiply(chosen, t_hi, t_lo, orb * orb, -orb * orb, rest * orb, cross)
    far_rest = lax.ppermute(far_rest, "tens", swap)

    beyond = prep_n(n_far, orb)
    o_main, o_rest = contract([own_main, own_rest], p_rows + early, [near, beyond], [(0, p_rows), (0, early)],
                              band, [orb, rest])
    oa = send(o_main, lambda t, s: (t, s - 1 + 2 * t))
    ob = send(o_main, lambda t, s: (1 - t, s - 1 + 2 * t))
    oc = send(o_rest, lambda t, s: (1 - t, s))
    r_main, = contract([far_main], cross, [near], [(early, cross)], band, [orb], after=(o_rest,))
    ra = send(r_main, lambda t, s: (t, s + 1 - 2 * t))
    rb = send(r_main, lambda t, s: (1 - t, s + 1 - 2 * t))
    r_rest, = contract([far_rest], cross, [near], [(early, cross)], band, [rest])
    rc = send(r_rest, lambda t, s: (1 - t, s))
    return finish((o_rest, oa, ob, oc), (r_rest, ra, rb, rc), orb, band)


def general(chibar, t_blocks, n_saved, q_list, q_count):
    tens = lax.axis_size("tens")
    t = lax.axis_index("tens")
    p_rows, n_cols = n_saved.shape
    blk = t_blocks.shape[0] // q_list.shape[-1]
    ql = q_list.shape[-1]
    qb = chibar.shape[1] // blk
    reach = REACH
    orb = int(round((n_cols // 3) ** 0.5))
    band = 3 * orb
    nu_t = t_blocks.shape[1] // orb
    high = lax.Precision.HIGH
    slot_ids = q_list.reshape(ql)
    in_use = q_count.reshape(())
    keeper = jnp.arange(ql) < in_use

    def chosen_of(r):
        rows = lax.dynamic_slice_in_dim(chibar, ((t + r) % tens) * p_rows, p_rows, 0)
        pieces = [rows if o == 0 else shift(rows, -o) for o in range(-reach, reach + 1)]
        blocks = [pc[:, b * blk:(b + 1) * blk] for pc in pieces for b in range(qb)]
        out = []
        for q in range(ql):
            pick = blocks[0]
            for i in range(1, len(blocks)):
                pick = jnp.where(slot_ids[q] == i, blocks[i], pick)
            out.append(jnp.where(keeper[q], pick, 0.0))
        return jnp.concatenate(out, axis=1)

    saved = n_saved.reshape(p_rows, orb, band)
    parts = []
    mb = []
    for r in list(range(1, tens)) + [0]:
        m = jnp.dot(chosen_of(r), t_blocks, precision=high, preferred_element_type=jnp.float32)
        if r:
            m = lax.ppermute(m, "tens", [(i, (i + r) % tens) for i in range(tens)])
        mb.append(m)
    mb = [mb[-1]] + mb[:-1]
    for r in range(tens):
        parts.append(jnp.einsum("pnm,pml->nl", mb[r].reshape(p_rows, nu_t, orb), saved, precision=high,
                                preferred_element_type=jnp.float32))
    stacked = jnp.stack(parts)
    order = (t - jnp.arange(tens)) % tens
    if tens == 2:
        partial = jnp.where(t == 0, stacked, stacked[::-1]).reshape(band, band)
    else:
        partial = jnp.take(stacked, order, axis=0).reshape(band, band)
    blocks = partial.reshape(3, orb, band)
    lower = shift(blocks[2], 1)
    upper = shift(blocks[0], -1)
    pad = lambda x, o: jnp.pad(x, ((0, 0), (o * orb, (2 - o) * orb)))
    res = pad(lower, 0) + pad(blocks[1], 1) + pad(upper, 2)
    if tens == 2:
        return res + lax.ppermute(res, "tens", [(0, 1), (1, 0)])
    return lax.psum(res, "tens")


def solution(mesh):
    placed = (
        P(None, "atom"),
        P(None, ("tens", "atom")),
        P("tens", "atom"),
        P("tens", "atom", None),
        P("tens", "atom"),
    )

    def program(body):
        return jax.shard_map(body, mesh=mesh, in_specs=placed, out_specs=P("atom", None), check_vma=False)

    if mesh.shape["tens"] != 2:
        return program(general)

    return program(paired)
```

```python
import jax
import jax.numpy as jnp
from jax import lax
from jax.experimental import pallas as pl
from jax.experimental.pallas import tpu as pltpu
from jax.sharding import PartitionSpec as P


LANES = 128
SUBL = 8
REACH = 3
ORDER = (-3, -2, -1, 3, 2, 1)
VM = pl.BlockSpec(memory_space=pltpu.VMEM)
HB = pl.BlockSpec(memory_space=pltpu.HBM)
f32 = jnp.float32
bf16 = jnp.bfloat16


def limit(mib):
    return pltpu.CompilerParams(vmem_limit_bytes=mib * 2**20)


def vmem(shape, dtype):
    return pltpu.VMEM(shape, dtype)


def split(x):
    hi = x.astype(bf16)
    return hi, (x - hi.astype(f32)).astype(bf16)


def shift(x, by):
    atoms = lax.axis_size("atom")
    return lax.ppermute(x, "atom", [(i, (i + by) % atoms) for i in range(atoms)])


def send(x, to):
    atoms = lax.axis_size("atom")
    pairs = []
    for t in range(2):
        for s in range(atoms):
            u, v = to(t, s)
            pairs.append((t * atoms + s, u * atoms + v % atoms))
    return lax.ppermute(x, ("tens", "atom"), pairs)


def prep_t(t_blocks, first, slope, cols):
    rows = t_blocks.shape[0]
    step = 64
    sub = 512 if cols % 512 == 0 else LANES

    def body(src, hi, lo, buf, sems):
        start = pl.multiple_of(first + slope * lax.axis_index("tens"), LANES)
        copies = []
        for i in range(rows // step):
            here = pl.ds(i * step, step)
            copies.append(pltpu.make_async_copy(src.at[here, pl.ds(start, cols)], buf.at[here], sems.at[i]))
            copies[-1].start()
        for i in range(rows // step):
            copies[i].wait()

            def tile(c, carry, i=i):
                at = pl.ds(pl.multiple_of(c * sub, sub), sub)
                here = pl.ds(i * step, step)
                h, l = split(buf[here, at])
                hi[here, at] = h
                lo[here, at] = l
                return carry

            lax.fori_loop(0, cols // sub, tile, 0)

    return pl.pallas_call(
        body, in_specs=[HB], out_specs=[VM, VM],
        out_shape=[vmem((rows, cols), bf16), vmem((rows, cols), bf16)],
        scratch_shapes=[pltpu.VMEM((rows, cols), f32), pltpu.SemaphoreType.DMA((rows // step,))],
        name="prep_t", compiler_params=limit(12),
    )(t_blocks)


def head(x, rows):
    def body(src, out, sem):
        copy = pltpu.make_async_copy(src.at[pl.ds(0, rows)], out, sem)
        copy.start()
        copy.wait()

    return pl.pallas_call(
        body, in_specs=[HB], out_specs=VM, out_shape=vmem((rows, x.shape[1]), x.dtype),
        scratch_shapes=[pltpu.SemaphoreType.DMA], name="head", compiler_params=limit(4),
    )(x)


def prep_n(saved, orb):
    rows, cols = saved.shape
    groups = rows // SUBL
    half = LANES // 2
    pairs = orb // 2
    wide = 2 * LANES

    def body(src, hi, lo, buf, tiles, tmp, sems):
        def copy(i):
            here = pl.ds(pl.multiple_of(i * SUBL, SUBL), SUBL)
            return pltpu.make_async_copy(src.at[here], buf.at[here], sems.at[i])

        for i in range(groups):
            copy(i).start()
        low = lax.broadcasted_iota(jnp.int32, (pairs, LANES), 1) < half

        def group(i, carry):
            copy(i).wait()
            here = pl.ds(pl.multiple_of(i * SUBL, SUBL), SUBL)
            for c in range(cols // LANES):
                tiles[c * SUBL:(c + 1) * SUBL, :] = buf[here, c * LANES:(c + 1) * LANES]
            for r in range(SUBL):
                v = [tiles[pl.ds(k * SUBL + r, pairs, stride=3 * SUBL), :] for k in range(3)]
                w1, w2 = (pltpu.roll(x, half, 1) for x in v[1:])
                tmp[r, 0, pl.ds(0, pairs, stride=2), :] = v[0]
                tmp[r, 1, pl.ds(0, pairs, stride=2), :] = v[1]
                tmp[r, 0, pl.ds(1, pairs, stride=2), :] = jnp.where(low, w1, w2)
                tmp[r, 1, pl.ds(1, pairs, stride=2), :] = w2
                at = pl.ds(pl.multiple_of(i * SUBL * orb + r * orb, orb), orb)
                for k in range(2):
                    h, l = split(tmp[r, k])
                    hi[at, k * LANES:(k + 1) * LANES] = h
                    lo[at, k * LANES:(k + 1) * LANES] = l
            return carry

        lax.fori_loop(0, groups, group, 0)

    return pl.pallas_call(
        body, in_specs=[HB], out_specs=[VM, VM],
        out_shape=[vmem((rows * orb, wide), bf16)] * 2,
        scratch_shapes=[pltpu.VMEM((rows, cols), f32), pltpu.VMEM((cols // LANES * SUBL, LANES), f32),
                        pltpu.VMEM((SUBL, 2, orb, LANES), f32), pltpu.SemaphoreType.DMA((groups,))],
        name="prep_n", compiler_params=limit(10),
    )(saved)


def select(pieces, q_list, q_count, p_rows, early):
    p_all, width = pieces[0].shape
    ql = q_list.shape[-1]
    blk = LANES
    qb = width // blk

    def body(*refs):
        parts, (list_ref, count_ref, out, scr) = refs[:len(pieces)], refs[len(pieces):]
        t = lax.axis_index("tens")
        for q in range(ql):
            used = jnp.where(count_ref[...] > q, list_ref[0][:, q:q + 1], -1)
            want = jnp.broadcast_to(used, (1, blk))
            pick = jnp.zeros((p_all, blk), f32)
            for i in range(len(parts) * qb):
                pick = jnp.where(want == i, parts[i // qb][:, (i % qb) * blk:(i % qb + 1) * blk], pick)
            scr[:, q * blk:(q + 1) * blk] = pick
        other = (1 - t) * p_rows
        order = ((other + early, p_rows - early), (t * p_rows, p_rows), (other, early))
        at = 0
        for start, size in order:
            h, l = split(scr[pl.ds(pl.multiple_of(start, 16), size), :])
            out[at:at + size, :] = h
            out[p_all + at:p_all + at + size, :] = l
            at += size

    return pl.pallas_call(
        body, in_specs=[VM] * (len(pieces) + 2), out_specs=VM,
        out_shape=vmem((2 * p_all, ql * blk), bf16),
        scratch_shapes=[pltpu.VMEM((p_all, ql * blk), f32)], name="select", compiler_params=limit(8),
    )(*pieces, q_list, q_count)


def multiply(chosen, t_parts, cross):
    p_all = chosen.shape[0] // 2
    cols = t_parts[0].shape[1]
    own = p_all - cross
    ct = cols // LANES
    sub = 512 if cols % 512 == 0 else 256

    def body(c, hi, lo, out_c, out_o):
        for j in range(cols // sub):
            at = pl.ds(j * sub, sub)
            big = jnp.dot(c[...], hi[:, at], preferred_element_type=f32)
            val = big[:p_all] + big[p_all:] + jnp.dot(c[:p_all, :], lo[:, at], preferred_element_type=f32)
            for k in range(sub // LANES):
                jt = j * (sub // LANES) + k
                for i in range(p_all // SUBL):
                    v = val[i * SUBL:(i + 1) * SUBL, k * LANES:(k + 1) * LANES]
                    if i < cross // SUBL:
                        out_c[pl.ds((i * ct + jt) * SUBL, SUBL), :] = v
                    else:
                        out_o[pl.ds(((i - cross // SUBL) * ct + jt) * SUBL, SUBL), :] = v

    return pl.pallas_call(
        body, in_specs=[VM] * 3, out_specs=[VM, VM],
        out_shape=[vmem((cross * ct, LANES), f32), vmem((own * ct, LANES), f32)], name="multiply", compiler_params=limit(8),
    )(chosen, *t_parts)


def contract_into(x, rows, ct, n_parts, n_rows, l_hi, l_lo):
    lane = lax.broadcasted_iota(jnp.int32, (ct, LANES), 1)
    low = lane < LANES // 2
    for p in range(0, rows, 2):
        a, b = (x[pl.ds((q // SUBL) * ct * SUBL + q % SUBL, ct, stride=SUBL), :] for q in (p, p + 1))
        even = jnp.where(low, a, pltpu.roll(b, LANES // 2, 1))
        odd = jnp.where(low, pltpu.roll(a, LANES // 2, 1), b)
        at = pl.ds((p // 2) * LANES, LANES)
        for i, v in enumerate((even, odd)):
            h, l = split(v)
            l_hi[pl.ds(i * ct, ct), at] = h
            l_lo[pl.ds(i * ct, ct), at] = l
    half = LANES // 2
    total = None
    at = 0
    for (w_hi, w_lo), (start, count) in zip(n_parts, n_rows):
        k = pl.ds(at * half, count * half)
        w = pl.ds(start * half, count * half)
        v = jnp.dot(l_hi[:, k], w_hi[w, :], preferred_element_type=f32)
        v += jnp.dot(l_lo[:, k], w_hi[w, :], preferred_element_type=f32)
        v += jnp.dot(l_hi[:, k], w_lo[w, :], preferred_element_type=f32)
        total = v if total is None else total + v
        at += count
    return total


def contract(stretches, rows, saved, n_rows, band, sizes, after=()):
    wide = -(-band // LANES)
    cts = [x.shape[0] // rows for x in stretches]
    flat = [w for pair in saved for w in pair]

    def body(*refs):
        refs = list(refs)
        xs = [refs.pop(0) for _ in stretches]
        ws = [refs.pop(0) for _ in flat]
        del refs[:len(after)]
        outs = [refs.pop(0) for _ in sizes]
        acc = refs.pop(0)
        pairs = list(zip(ws[0::2], ws[1::2]))
        base = 0
        for i, (x, ct) in enumerate(zip(xs, cts)):
            val = contract_into(x, rows, ct, pairs, n_rows, refs[2 * i], refs[2 * i + 1])
            for par in range(2):
                for c in range(wide):
                    acc[c, pl.ds(base + par, ct, stride=2), :] = val[par * ct:(par + 1) * ct, c * LANES:(c + 1) * LANES]
            base += 2 * ct
        at = 0
        for out, size in zip(outs, sizes):
            out[...] = jnp.concatenate([acc[c, at:at + size, :] for c in range(wide)], axis=1)[:, :band]
            at += size

    scratch = [pltpu.VMEM((wide, 2 * sum(cts), LANES), f32)]
    for x, ct in zip(stretches, cts):
        scratch += [pltpu.VMEM((2 * ct, rows * LANES // 2), bf16)] * 2
    return pl.pallas_call(
        body, in_specs=[VM] * (len(stretches) + len(flat) + len(after)), out_specs=[VM] * len(sizes),
        out_shape=[vmem((size, band), f32) for size in sizes], scratch_shapes=scratch,
        name="contract", compiler_params=limit(12),
    )(*stretches, *flat, *after)


def finish(own, rec, orb, band):
    def body(ho, oa, ob, oc, hr, ra, rb, rc, out):
        t = lax.axis_index("tens")
        first = t == 0
        lower = jnp.where(first, ob[...], oa[...]) + jnp.where(first, ra[...], rb[...])
        upper = jnp.where(first, oa[...], ob[...]) + jnp.where(first, rb[...], ra[...])
        x = ho[...] + rc[...]
        y = oc[...] + hr[...]
        mid = jnp.concatenate([jnp.where(first, x, y), jnp.where(first, y, x)], axis=0)
        zero = jnp.zeros((orb, orb), f32)
        out[...] = (jnp.concatenate([lower, zero, zero], axis=1) + jnp.concatenate([zero, mid, zero], axis=1)
                    + jnp.concatenate([zero, zero, upper], axis=1))

    return pl.pallas_call(
        body, in_specs=[VM] * 8, out_specs=VM,
        out_shape=jax.ShapeDtypeStruct((orb, band + 2 * orb), f32), name="finish", compiler_params=limit(8),
    )(*own, *rec)


def paired(chibar, t_blocks, n_saved, q_list, q_count):
    p_rows, n_cols = n_saved.shape
    orb = LANES // 2
    band = n_cols // orb
    nu_t = t_blocks.shape[1] // orb
    early = 16
    cross = p_rows - early
    swap = [(0, 1), (1, 0)]

    n_saved = pltpu.with_memory_space_constraint(n_saved, pltpu.HBM)
    t_blocks = pltpu.with_memory_space_constraint(t_blocks, pltpu.HBM)
    n_far = lax.ppermute(head(n_saved, early), "tens", swap)
    moved = {o: shift(chibar, -o) for o in ORDER}
    pieces = [moved[o] if o else chibar for o in range(-REACH, REACH + 1)]
    rest = nu_t - orb
    t_main = prep_t(t_blocks, 0, rest * orb, orb * orb)
    chosen = select(pieces, q_list, q_count, p_rows, early)
    far_main, own_main = multiply(chosen, t_main, cross)
    far_main = lax.ppermute(far_main, "tens", swap)
    t_rest = prep_t(t_blocks, orb * orb, -orb * orb, rest * orb)
    far_rest, own_rest = multiply(chosen, t_rest, cross)
    far_rest = lax.ppermute(far_rest, "tens", swap)

    near = prep_n(n_saved, orb)
    beyond = prep_n(n_far, orb)
    o_main, o_rest = contract([own_main, own_rest], p_rows + early, [near, beyond], [(0, p_rows), (0, early)],
                              band, [orb, rest])
    oa = send(o_main, lambda t, s: (t, s - 1 + 2 * t))
    ob = send(o_main, lambda t, s: (1 - t, s - 1 + 2 * t))
    oc = send(o_rest, lambda t, s: (1 - t, s))
    r_main, = contract([far_main], cross, [near], [(early, cross)], band, [orb], after=(o_rest,))
    ra = send(r_main, lambda t, s: (t, s + 1 - 2 * t))
    rb = send(r_main, lambda t, s: (1 - t, s + 1 - 2 * t))
    r_rest, = contract([far_rest], cross, [near], [(early, cross)], band, [rest])
    rc = send(r_rest, lambda t, s: (1 - t, s))
    return finish((o_rest, oa, ob, oc), (r_rest, ra, rb, rc), orb, band)


def general(chibar, t_blocks, n_saved, q_list, q_count):
    tens = lax.axis_size("tens")
    t = lax.axis_index("tens")
    p_rows, n_cols = n_saved.shape
    blk = t_blocks.shape[0] // q_list.shape[-1]
    ql = q_list.shape[-1]
    qb = chibar.shape[1] // blk
    reach = REACH
    orb = int(round((n_cols // 3) ** 0.5))
    band = 3 * orb
    nu_t = t_blocks.shape[1] // orb
    high = lax.Precision.HIGH
    slot_ids = q_list.reshape(ql)
    in_use = q_count.reshape(())
    keeper = jnp.arange(ql) < in_use

    def chosen_of(r):
        rows = lax.dynamic_slice_in_dim(chibar, ((t + r) % tens) * p_rows, p_rows, 0)
        pieces = [rows if o == 0 else shift(rows, -o) for o in range(-reach, reach + 1)]
        blocks = [pc[:, b * blk:(b + 1) * blk] for pc in pieces for b in range(qb)]
        out = []
        for q in range(ql):
            pick = blocks[0]
            for i in range(1, len(blocks)):
                pick = jnp.where(slot_ids[q] == i, blocks[i], pick)
            out.append(jnp.where(keeper[q], pick, 0.0))
        return jnp.concatenate(out, axis=1)

    saved = n_saved.reshape(p_rows, orb, band)
    parts = []
    mb = []
    for r in list(range(1, tens)) + [0]:
        m = jnp.dot(chosen_of(r), t_blocks, precision=high, preferred_element_type=jnp.float32)
        if r:
            m = lax.ppermute(m, "tens", [(i, (i + r) % tens) for i in range(tens)])
        mb.append(m)
    mb = [mb[-1]] + mb[:-1]
    for r in range(tens):
        parts.append(jnp.einsum("pnm,pml->nl", mb[r].reshape(p_rows, nu_t, orb), saved, precision=high,
                                preferred_element_type=jnp.float32))
    stacked = jnp.stack(parts)
    order = (t - jnp.arange(tens)) % tens
    if tens == 2:
        partial = jnp.where(t == 0, stacked, stacked[::-1]).reshape(band, band)
    else:
        partial = jnp.take(stacked, order, axis=0).reshape(band, band)
    blocks = partial.reshape(3, orb, band)
    lower = shift(blocks[2], 1)
    upper = shift(blocks[0], -1)
    pad = lambda x, o: jnp.pad(x, ((0, 0), (o * orb, (2 - o) * orb)))
    res = pad(lower, 0) + pad(blocks[1], 1) + pad(upper, 2)
    if tens == 2:
        return res + lax.ppermute(res, "tens", [(0, 1), (1, 0)])
    return lax.psum(res, "tens")


def solution(mesh):
    placed = (
        P(None, "atom"),
        P(None, ("tens", "atom")),
        P("tens", "atom"),
        P("tens", "atom", None),
        P("tens", "atom"),
    )

    def program(body):
        return jax.shard_map(body, mesh=mesh, in_specs=placed, out_specs=P("atom", None), check_vma=False)

    if mesh.shape["tens"] != 2:
        return program(general)

    return program(paired)
```

```python
import jax
import jax.numpy as jnp
from jax import lax
from jax.experimental import pallas as pl
from jax.experimental.pallas import tpu as pltpu
from jax.sharding import PartitionSpec as P


LANES = 128
SUBL = 8
REACH = 3
EARLY_PART = 8
VM = pl.BlockSpec(memory_space=pltpu.VMEM)
HB = pl.BlockSpec(memory_space=pltpu.HBM)
f32 = jnp.float32
bf16 = jnp.bfloat16


def limit(mib):
    return pltpu.CompilerParams(vmem_limit_bytes=mib * 2**20)


def vmem(shape, dtype):
    return pltpu.VMEM(shape, dtype)


def split(x):
    hi = x.astype(bf16)
    return hi, (x - hi.astype(f32)).astype(bf16)


def shift(x, by):
    atoms = lax.axis_size("atom")
    return lax.ppermute(x, "atom", [(i, (i + by) % atoms) for i in range(atoms)])


def send(x, to):
    atoms = lax.axis_size("atom")
    pairs = []
    for t in range(2):
        for s in range(atoms):
            u, v = to(t, s)
            pairs.append((t * atoms + s, u * atoms + v % atoms))
    return lax.ppermute(x, ("tens", "atom"), pairs)


def neighbours(x):
    atoms = lax.axis_size("atom")
    pair = [(i, i ^ 1) for i in range(atoms)]

    def move(y, pairs):
        return lax.ppermute(y, "atom", pairs)

    far = move(x, [(i, (i + (3 if i % 2 else -3)) % atoms) for i in range(atoms)])
    below = move(x, [(i, (i + 2) % atoms) for i in range(atoms)])
    above = move(x, [(i, (i - 2) % atoms) for i in range(atoms)])
    partner = move(x, pair)
    return [far, below, move(below, pair), x, partner, above, move(above, pair)]


def prep_t(t_blocks, first, slope, cols, *early):
    rows = t_blocks.shape[0]
    step = 64
    sub = 512 if cols % 512 == 0 else LANES

    def body(src, *refs):
        hi, lo, buf, sems = refs[len(early):]
        start = pl.multiple_of(first + slope * lax.axis_index("tens"), LANES)
        copies = []
        for i in range(rows // step):
            here = pl.ds(i * step, step)
            copies.append(pltpu.make_async_copy(src.at[here, pl.ds(start, cols)], buf.at[here], sems.at[i]))
            copies[-1].start()
        for i in range(rows // step):
            copies[i].wait()

            def tile(c, carry, i=i):
                at = pl.ds(pl.multiple_of(c * sub, sub), sub)
                here = pl.ds(i * step, step)
                h, l = split(buf[here, at])
                hi[here, at] = h
                lo[here, at] = l
                return carry

            lax.fori_loop(0, cols // sub, tile, 0)

    return pl.pallas_call(
        body, in_specs=[HB] + [VM] * len(early), out_specs=[VM, VM],
        out_shape=[vmem((rows, cols), bf16), vmem((rows, cols), bf16)],
        scratch_shapes=[pltpu.VMEM((rows, cols), f32), pltpu.SemaphoreType.DMA((rows // step,))],
        name="prep_t", compiler_params=limit(12),
    )(t_blocks, *early)


def head(x, part):
    tiles = x.shape[1] // LANES
    rows = 2 * SUBL

    def body(src, out, buf, sem):
        copy = pltpu.make_async_copy(src.at[pl.ds(0, rows)], buf, sem)
        copy.start()
        copy.wait()
        for c in range(tiles):
            at = pl.ds(c * LANES, LANES)
            out[pl.ds(c * SUBL, SUBL), :] = buf[:SUBL, at]
            out[pl.ds(tiles * SUBL + c * part, part), :] = buf[SUBL:SUBL + part, at]

    return pl.pallas_call(
        body, in_specs=[HB], out_specs=VM, out_shape=vmem((tiles * (SUBL + part), LANES), x.dtype),
        scratch_shapes=[pltpu.VMEM((rows, x.shape[1]), f32), pltpu.SemaphoreType.DMA],
        name="head", compiler_params=limit(4),
    )(x)


def place_row(tiles, first, per, orb, tmp, hi, lo, at):
    half = LANES // 2
    pairs = orb // 2
    low = lax.broadcasted_iota(jnp.int32, (pairs, LANES), 1) < half
    v = [tiles[pl.ds(first + k * per, pairs, stride=3 * per), :] for k in range(3)]
    w1, w2 = (pltpu.roll(x, half, 1) for x in v[1:])
    tmp[0, pl.ds(0, pairs, stride=2), :] = v[0]
    tmp[1, pl.ds(0, pairs, stride=2), :] = v[1]
    tmp[0, pl.ds(1, pairs, stride=2), :] = jnp.where(low, w1, w2)
    tmp[1, pl.ds(1, pairs, stride=2), :] = w2
    for k in range(2):
        h, l = split(tmp[k])
        hi[at, k * LANES:(k + 1) * LANES] = h
        lo[at, k * LANES:(k + 1) * LANES] = l


def prep_n(saved, orb):
    rows, cols = saved.shape
    groups = rows // SUBL

    def body(src, hi, lo, buf, tiles, tmp, sems):
        def copy(i):
            here = pl.ds(pl.multiple_of(i * SUBL, SUBL), SUBL)
            return pltpu.make_async_copy(src.at[here], buf.at[here], sems.at[i])

        for i in range(groups):
            copy(i).start()

        def group(i, carry):
            copy(i).wait()
            here = pl.ds(pl.multiple_of(i * SUBL, SUBL), SUBL)
            for c in range(cols // LANES):
                tiles[c * SUBL:(c + 1) * SUBL, :] = buf[here, c * LANES:(c + 1) * LANES]
            for r in range(SUBL):
                at = pl.ds(pl.multiple_of(i * SUBL * orb + r * orb, orb), orb)
                place_row(tiles, r, SUBL, orb, tmp.at[r], hi, lo, at)
            return carry

        lax.fori_loop(0, groups, group, 0)

    return pl.pallas_call(
        body, in_specs=[HB], out_specs=[VM, VM],
        out_shape=[vmem((rows * orb, 2 * LANES), bf16)] * 2,
        scratch_shapes=[pltpu.VMEM((rows, cols), f32), pltpu.VMEM((cols // LANES * SUBL, LANES), f32),
                        pltpu.VMEM((SUBL, 2, orb, LANES), f32), pltpu.SemaphoreType.DMA((groups,))],
        name="prep_n", compiler_params=limit(10),
    )(saved)


def prep_far(packed, part, orb):
    rows = SUBL + part
    tiles = packed.shape[0] // rows

    def body(src, hi, lo, tmp):
        for p in range(rows):
            first, per = (p, SUBL) if p < SUBL else (tiles * SUBL + p - SUBL, part)
            place_row(src, first, per, orb, tmp.at[p], hi, lo, pl.ds(p * orb, orb))

    return pl.pallas_call(
        body, in_specs=[VM], out_specs=[VM, VM], out_shape=[vmem((rows * orb, 2 * LANES), bf16)] * 2,
        scratch_shapes=[pltpu.VMEM((rows, 2, orb, LANES), f32)], name="prep_far", compiler_params=limit(6),
    )(packed)


def select(pieces, q_list, q_count, p_rows, early):
    p_all, width = pieces[0].shape
    ql = q_list.shape[-1]
    blk = LANES
    qb = width // blk

    def body(*refs):
        parts, (list_ref, count_ref, out, scr) = refs[:len(pieces)], refs[len(pieces):]
        t = lax.axis_index("tens")
        s = lax.axis_index("atom")
        for q in range(ql):
            used = jnp.where(count_ref[...] > q, list_ref[0][:, q:q + 1], -1)
            turned = (((used >> 1) & 1) == 0) & (s % 2 == 1)
            used = jnp.where(turned, 2 * (((used >> 1) + 2) & 7) + (used & 1), used)
            want = jnp.broadcast_to(used, (1, blk))
            pick = jnp.zeros((p_all, blk), f32)
            for i in range(len(parts) * qb):
                pick = jnp.where(want == i, parts[i // qb][:, (i % qb) * blk:(i % qb + 1) * blk], pick)
            scr[:, q * blk:(q + 1) * blk] = pick
        other = (1 - t) * p_rows
        order = ((other + early, p_rows - early), (t * p_rows, p_rows), (other, early))
        at = 0
        for start, size in order:
            h, l = split(scr[pl.ds(pl.multiple_of(start, 16), size), :])
            out[at:at + size, :] = h
            out[p_all + at:p_all + at + size, :] = l
            at += size

    return pl.pallas_call(
        body, in_specs=[VM] * (len(pieces) + 2), out_specs=VM,
        out_shape=vmem((2 * p_all, ql * blk), bf16),
        scratch_shapes=[pltpu.VMEM((p_all, ql * blk), f32)], name="select", compiler_params=limit(8),
    )(*pieces, q_list, q_count)


def multiply(chosen, t_parts, p_rows, part):
    p_all = chosen.shape[0] // 2
    cols = t_parts[0][0].shape[1]
    ct = cols * len(t_parts) // LANES
    sub = 512 if cols % 512 == 0 else 256
    far_full = p_rows // SUBL - 2
    own_full = p_all // SUBL - far_full - 1

    def body(c, *refs):
        out_c, out_o = refs[-2:]
        for j in range(cols * len(t_parts) // sub):
            which = j * sub // cols
            hi, lo = refs[2 * which:2 * which + 2]
            at = pl.ds(j * sub - which * cols, sub)
            big = jnp.dot(c[...], hi[:, at], preferred_element_type=f32)
            val = big[:p_all] + big[p_all:] + jnp.dot(c[:p_all, :], lo[:, at], preferred_element_type=f32)
            for k in range(sub // LANES):
                jt = j * (sub // LANES) + k
                for i in range(p_all // SUBL):
                    v = val[i * SUBL:(i + 1) * SUBL, k * LANES:(k + 1) * LANES]
                    if i < far_full:
                        out_c[pl.ds((i * ct + jt) * SUBL, SUBL), :] = v
                    elif i < far_full + own_full:
                        out_o[pl.ds(((i - far_full) * ct + jt) * SUBL, SUBL), :] = v
                    else:
                        out_o[pl.ds(own_full * ct * SUBL + jt * part, part), :] = v[:part]
                        rest = SUBL - part
                        if rest:
                            out_c[pl.ds(far_full * ct * SUBL + jt * rest, rest), :] = v[part:]

    return pl.pallas_call(
        body, in_specs=[VM] * (1 + 2 * len(t_parts)), out_specs=[VM, VM],
        out_shape=[vmem(((far_full * SUBL + SUBL - part) * ct, LANES), f32),
                   vmem(((own_full * SUBL + part) * ct, LANES), f32)],
        name="multiply", compiler_params=limit(8),
    )(chosen, *[x for part in t_parts for x in part])


def contract_into(x, rows, ct, n_parts, n_rows, left):
    lane = lax.broadcasted_iota(jnp.int32, (ct, LANES), 1)
    low = lane < LANES // 2
    tail = rows % SUBL

    def row(q):
        per = SUBL if q < rows - tail else tail
        return x[pl.ds((q // SUBL) * ct * SUBL + q % SUBL, ct, stride=per), :]

    for p in range(0, rows, 2):
        a, b = row(p), row(p + 1)
        even = jnp.where(low, a, pltpu.roll(b, LANES // 2, 1))
        odd = jnp.where(low, pltpu.roll(a, LANES // 2, 1), b)
        at = pl.ds((p // 2) * LANES, LANES)
        for i, v in enumerate((even, odd)):
            h, l = split(v)
            left[pl.ds(i * ct, ct), at] = h
            left[pl.ds((2 + i) * ct, ct), at] = l
    half = LANES // 2
    total = None
    at = 0
    for (w_hi, w_lo), (start, count) in zip(n_parts, n_rows):
        k = pl.ds(at * half, count * half)
        w = pl.ds(start * half, count * half)
        both = jnp.dot(left[:, k], w_hi[w, :], preferred_element_type=f32)
        v = both[:2 * ct] + both[2 * ct:]
        v += jnp.dot(left[:2 * ct, k], w_lo[w, :], preferred_element_type=f32)
        total = v if total is None else total + v
        at += count
    return total


def contract(stretches, rows, saved, n_rows, band, sizes, after=()):
    wide = -(-band // LANES)
    cts = [x.shape[0] // rows for x in stretches]
    flat = [w for pair in saved for w in pair]

    def body(*refs):
        refs = list(refs)
        xs = [refs.pop(0) for _ in stretches]
        ws = [refs.pop(0) for _ in flat]
        del refs[:len(after)]
        outs = [refs.pop(0) for _ in sizes]
        acc = refs.pop(0)
        pairs = list(zip(ws[0::2], ws[1::2]))
        base = 0
        for i, (x, ct) in enumerate(zip(xs, cts)):
            val = contract_into(x, rows, ct, pairs, n_rows, refs[i])
            for par in range(2):
                for c in range(wide):
                    acc[c, pl.ds(base + par, ct, stride=2), :] = val[par * ct:(par + 1) * ct, c * LANES:(c + 1) * LANES]
            base += 2 * ct
        at = 0
        for out, size in zip(outs, sizes):
            half = size // 2
            low = lax.broadcasted_iota(jnp.int32, (half, LANES), 1) < LANES // 2
            out[:size, :] = acc[0, at:at + size, :]
            out[size:, :] = jnp.where(low, acc[1, at:at + half, :], pltpu.roll(acc[1, at + half:at + size, :], LANES // 2, 1))
            at += size

    scratch = [pltpu.VMEM((wide, 2 * sum(cts), LANES), f32)]
    for x, ct in zip(stretches, cts):
        scratch.append(pltpu.VMEM((4 * ct, rows * LANES // 2), bf16))
    return pl.pallas_call(
        body, in_specs=[VM] * (len(stretches) + len(flat) + len(after)), out_specs=[VM] * len(sizes),
        out_shape=[vmem((size * band // LANES, LANES), f32) for size in sizes], scratch_shapes=scratch,
        name="contract", compiler_params=limit(12),
    )(*stretches, *flat, *after)


def unpack(x, size, band):
    low = x[size:]
    tail = jnp.concatenate([low, pltpu.roll(low, LANES // 2, 1)], axis=0)
    return jnp.concatenate([x[:size], tail], axis=1)[:, :band]


def finish(own, rec, orb, band):
    def body(ho, oa, ob, oc, hr, ra, rb, rc, out):
        first = lax.axis_index("tens") == 0
        lower = jnp.where(first, ob[...], oa[...]) + jnp.where(first, ra[...], rb[...])
        upper = jnp.where(first, oa[...], ob[...]) + jnp.where(first, rb[...], ra[...])
        x = ho[...] + rc[...]
        y = oc[...] + hr[...]
        rest = x.shape[0] * LANES // band
        x, y = unpack(jnp.where(first, x, y), rest, band), unpack(jnp.where(first, y, x), rest, band)
        lower, upper = unpack(lower, orb, band), unpack(upper, orb, band)
        zero = jnp.zeros((orb, orb), f32)
        out[...] = (jnp.concatenate([lower, zero, zero], axis=1)
                    + jnp.concatenate([zero, jnp.concatenate([x, y], axis=0), zero], axis=1)
                    + jnp.concatenate([zero, zero, upper], axis=1))

    return pl.pallas_call(
        body, in_specs=[VM] * 8, out_specs=VM,
        out_shape=jax.ShapeDtypeStruct((orb, band + 2 * orb), f32), name="finish", compiler_params=limit(8),
    )(*own, *rec)


def paired(chibar, t_blocks, n_saved, q_list, q_count):
    p_rows, n_cols = n_saved.shape
    orb = LANES // 2
    band = n_cols // orb
    nu_t = t_blocks.shape[1] // orb
    part = EARLY_PART
    early = SUBL + part
    cross = p_rows - early
    swap = [(0, 1), (1, 0)]

    n_saved = pltpu.with_memory_space_constraint(n_saved, pltpu.HBM)
    t_blocks = pltpu.with_memory_space_constraint(t_blocks, pltpu.HBM)
    n_far = lax.ppermute(head(n_saved, part), "tens", swap)
    pieces = neighbours(chibar)
    rest = nu_t - orb
    half = orb * orb // 2
    t_main = [prep_t(t_blocks, 0, rest * orb, half, q_count)]
    t_main.append(prep_t(t_blocks, half, rest * orb, half))
    chosen = select(pieces, q_list, q_count, p_rows, 2 * SUBL)
    far_main, own_main = multiply(chosen, t_main, p_rows, part)
    far_main = lax.ppermute(far_main, "tens", swap)
    t_rest = prep_t(t_blocks, orb * orb, -orb * orb, rest * orb)
    far_rest, own_rest = multiply(chosen, [t_rest], p_rows, part)
    far_rest = lax.ppermute(far_rest, "tens", swap)

    near = prep_n(n_saved, orb)
    beyond = prep_far(n_far, part, orb)
    far_rows = [(2 * SUBL, p_rows - 2 * SUBL), (early, SUBL - part)][:2 if part < SUBL else 1]
    o_main, o_rest = contract([own_main, own_rest], p_rows + early, [near, beyond], [(0, p_rows), (0, early)],
                              band, [orb, rest])
    oa = send(o_main, lambda t, s: (t, s - 1 + 2 * t))
    ob = send(o_main, lambda t, s: (1 - t, s - 1 + 2 * t))
    oc = send(o_rest, lambda t, s: (1 - t, s))
    r_main, = contract([far_main], cross, [near, near], far_rows, band, [orb], after=(o_rest,))
    ra = send(r_main, lambda t, s: (t, s + 1 - 2 * t))
    rb = send(r_main, lambda t, s: (1 - t, s + 1 - 2 * t))
    r_rest, = contract([far_rest], cross, [near, near], far_rows, band, [rest])
    rc = send(r_rest, lambda t, s: (1 - t, s))
    return finish((o_rest, oa, ob, oc), (r_rest, ra, rb, rc), orb, band)


def general(chibar, t_blocks, n_saved, q_list, q_count):
    tens = lax.axis_size("tens")
    t = lax.axis_index("tens")
    p_rows, n_cols = n_saved.shape
    blk = t_blocks.shape[0] // q_list.shape[-1]
    ql = q_list.shape[-1]
    qb = chibar.shape[1] // blk
    reach = REACH
    orb = int(round((n_cols // 3) ** 0.5))
    band = 3 * orb
    nu_t = t_blocks.shape[1] // orb
    high = lax.Precision.HIGH
    slot_ids = q_list.reshape(ql)
    in_use = q_count.reshape(())
    keeper = jnp.arange(ql) < in_use

    def chosen_of(r):
        rows = lax.dynamic_slice_in_dim(chibar, ((t + r) % tens) * p_rows, p_rows, 0)
        pieces = [rows if o == 0 else shift(rows, -o) for o in range(-reach, reach + 1)]
        blocks = [pc[:, b * blk:(b + 1) * blk] for pc in pieces for b in range(qb)]
        out = []
        for q in range(ql):
            pick = blocks[0]
            for i in range(1, len(blocks)):
                pick = jnp.where(slot_ids[q] == i, blocks[i], pick)
            out.append(jnp.where(keeper[q], pick, 0.0))
        return jnp.concatenate(out, axis=1)

    saved = n_saved.reshape(p_rows, orb, band)
    parts = []
    mb = []
    for r in list(range(1, tens)) + [0]:
        m = jnp.dot(chosen_of(r), t_blocks, precision=high, preferred_element_type=jnp.float32)
        if r:
            m = lax.ppermute(m, "tens", [(i, (i + r) % tens) for i in range(tens)])
        mb.append(m)
    mb = [mb[-1]] + mb[:-1]
    for r in range(tens):
        parts.append(jnp.einsum("pnm,pml->nl", mb[r].reshape(p_rows, nu_t, orb), saved, precision=high,
                                preferred_element_type=jnp.float32))
    stacked = jnp.stack(parts)
    order = (t - jnp.arange(tens)) % tens
    if tens == 2:
        partial = jnp.where(t == 0, stacked, stacked[::-1]).reshape(band, band)
    else:
        partial = jnp.take(stacked, order, axis=0).reshape(band, band)
    blocks = partial.reshape(3, orb, band)
    lower = shift(blocks[2], 1)
    upper = shift(blocks[0], -1)
    pad = lambda x, o: jnp.pad(x, ((0, 0), (o * orb, (2 - o) * orb)))
    res = pad(lower, 0) + pad(blocks[1], 1) + pad(upper, 2)
    if tens == 2:
        return res + lax.ppermute(res, "tens", [(0, 1), (1, 0)])
    return lax.psum(res, "tens")


def solution(mesh):
    placed = (
        P(None, "atom"),
        P(None, ("tens", "atom")),
        P("tens", "atom"),
        P("tens", "atom", None),
        P("tens", "atom"),
    )

    def program(body):
        return jax.shard_map(body, mesh=mesh, in_specs=placed, out_specs=P("atom", None), check_vma=False)

    if mesh.shape["tens"] != 2 or mesh.shape["atom"] % 2:
        return program(general)

    return program(paired)
```

```python
import jax
import jax.numpy as jnp
from jax import lax
from jax.experimental import pallas as pl
from jax.experimental.pallas import tpu as pltpu
from jax.sharding import PartitionSpec as P


LANES = 128
SUBL = 8
REACH = 3
EARLY_PART = 8
VM = pl.BlockSpec(memory_space=pltpu.VMEM)
HB = pl.BlockSpec(memory_space=pltpu.HBM)
f32 = jnp.float32
bf16 = jnp.bfloat16


def limit(mib):
    return pltpu.CompilerParams(vmem_limit_bytes=mib * 2**20)


def vmem(shape, dtype):
    return pltpu.VMEM(shape, dtype)


def split(x):
    hi = x.astype(bf16)
    return hi, (x - hi.astype(f32)).astype(bf16)


def shift(x, by):
    atoms = lax.axis_size("atom")
    return lax.ppermute(x, "atom", [(i, (i + by) % atoms) for i in range(atoms)])


def send(x, to):
    atoms = lax.axis_size("atom")
    pairs = []
    for t in range(2):
        for s in range(atoms):
            u, v = to(t, s)
            pairs.append((t * atoms + s, u * atoms + v % atoms))
    return lax.ppermute(x, ("tens", "atom"), pairs)


def neighbours(x):
    atoms = lax.axis_size("atom")
    pair = [(i, i ^ 1) for i in range(atoms)]

    def move(y, pairs):
        return lax.ppermute(y, "atom", pairs)

    far = move(x, [(i, (i + (3 if i % 2 else -3)) % atoms) for i in range(atoms)])
    below = move(x, [(i, (i + 2) % atoms) for i in range(atoms)])
    above = move(x, [(i, (i - 2) % atoms) for i in range(atoms)])
    partner = move(x, pair)
    return [far, below, move(below, pair), x, partner, above, move(above, pair)]


def prep_t(t_blocks, first, slope, cols, *early):
    rows = t_blocks.shape[0]
    step = 64
    sub = 512 if cols % 512 == 0 else LANES

    def body(src, *refs):
        hi, lo, buf, sems = refs[len(early):]
        start = pl.multiple_of(first + slope * lax.axis_index("tens"), LANES)
        copies = []
        for i in range(rows // step):
            here = pl.ds(i * step, step)
            copies.append(pltpu.make_async_copy(src.at[here, pl.ds(start, cols)], buf.at[here], sems.at[i]))
            copies[-1].start()
        for i in range(rows // step):
            copies[i].wait()

            def tile(c, carry, i=i):
                at = pl.ds(pl.multiple_of(c * sub, sub), sub)
                here = pl.ds(i * step, step)
                h, l = split(buf[here, at])
                hi[here, at] = h
                lo[here, at] = l
                return carry

            lax.fori_loop(0, cols // sub, tile, 0)

    return pl.pallas_call(
        body, in_specs=[HB] + [VM] * len(early), out_specs=[VM, VM],
        out_shape=[vmem((rows, cols), bf16), vmem((rows, cols), bf16)],
        scratch_shapes=[pltpu.VMEM((rows, cols), f32), pltpu.SemaphoreType.DMA((rows // step,))],
        name="prep_t", compiler_params=limit(12),
    )(t_blocks, *early)


def head(x, part):
    tiles = x.shape[1] // LANES
    rows = 2 * SUBL

    def body(src, out, buf, sem):
        copy = pltpu.make_async_copy(src.at[pl.ds(0, rows)], buf, sem)
        copy.start()
        copy.wait()
        for c in range(tiles):
            at = pl.ds(c * LANES, LANES)
            out[pl.ds(c * SUBL, SUBL), :] = buf[:SUBL, at]
            out[pl.ds(tiles * SUBL + c * part, part), :] = buf[SUBL:SUBL + part, at]

    return pl.pallas_call(
        body, in_specs=[HB], out_specs=VM, out_shape=vmem((tiles * (SUBL + part), LANES), x.dtype),
        scratch_shapes=[pltpu.VMEM((rows, x.shape[1]), f32), pltpu.SemaphoreType.DMA],
        name="head", compiler_params=limit(4),
    )(x)


def place_row(tiles, first, per, orb, tmp, hi, lo, at):
    half = LANES // 2
    pairs = orb // 2
    low = lax.broadcasted_iota(jnp.int32, (pairs, LANES), 1) < half
    v = [tiles[pl.ds(first + k * per, pairs, stride=3 * per), :] for k in range(3)]
    w1, w2 = (pltpu.roll(x, half, 1) for x in v[1:])
    tmp[0, pl.ds(0, pairs, stride=2), :] = v[0]
    tmp[1, pl.ds(0, pairs, stride=2), :] = v[1]
    tmp[0, pl.ds(1, pairs, stride=2), :] = jnp.where(low, w1, w2)
    tmp[1, pl.ds(1, pairs, stride=2), :] = w2
    for k in range(2):
        h, l = split(tmp[k])
        hi[at, k * LANES:(k + 1) * LANES] = h
        lo[at, k * LANES:(k + 1) * LANES] = l


def prep_n(saved, orb):
    rows, cols = saved.shape
    groups = rows // SUBL

    def body(src, hi, lo, buf, tiles, tmp, sems):
        def copy(i):
            here = pl.ds(pl.multiple_of(i * SUBL, SUBL), SUBL)
            return pltpu.make_async_copy(src.at[here], buf.at[here], sems.at[i])

        for i in range(groups):
            copy(i).start()

        def group(i, carry):
            copy(i).wait()
            here = pl.ds(pl.multiple_of(i * SUBL, SUBL), SUBL)
            for c in range(cols // LANES):
                tiles[c * SUBL:(c + 1) * SUBL, :] = buf[here, c * LANES:(c + 1) * LANES]
            for r in range(SUBL):
                at = pl.ds(pl.multiple_of(i * SUBL * orb + r * orb, orb), orb)
                place_row(tiles, r, SUBL, orb, tmp.at[r], hi, lo, at)
            return carry

        lax.fori_loop(0, groups, group, 0)

    return pl.pallas_call(
        body, in_specs=[HB], out_specs=[VM, VM],
        out_shape=[vmem((rows * orb, 2 * LANES), bf16)] * 2,
        scratch_shapes=[pltpu.VMEM((rows, cols), f32), pltpu.VMEM((cols // LANES * SUBL, LANES), f32),
                        pltpu.VMEM((SUBL, 2, orb, LANES), f32), pltpu.SemaphoreType.DMA((groups,))],
        name="prep_n", compiler_params=limit(10),
    )(saved)


def prep_far(packed, part, orb):
    rows = SUBL + part
    tiles = packed.shape[0] // rows

    def body(src, hi, lo, tmp):
        for p in range(rows):
            first, per = (p, SUBL) if p < SUBL else (tiles * SUBL + p - SUBL, part)
            place_row(src, first, per, orb, tmp.at[p], hi, lo, pl.ds(p * orb, orb))

    return pl.pallas_call(
        body, in_specs=[VM], out_specs=[VM, VM], out_shape=[vmem((rows * orb, 2 * LANES), bf16)] * 2,
        scratch_shapes=[pltpu.VMEM((rows, 2, orb, LANES), f32)], name="prep_far", compiler_params=limit(6),
    )(packed)


def select(pieces, q_list, q_count, p_rows, early):
    p_all, width = pieces[0].shape
    ql = q_list.shape[-1]
    blk = LANES
    qb = width // blk

    def body(*refs):
        parts, (list_ref, count_ref, out, scr) = refs[:len(pieces)], refs[len(pieces):]
        t = lax.axis_index("tens")
        s = lax.axis_index("atom")
        for q in range(ql):
            used = jnp.where(count_ref[...] > q, list_ref[0][:, q:q + 1], -1)
            turned = (((used >> 1) & 1) == 0) & (s % 2 == 1)
            used = jnp.where(turned, 2 * (((used >> 1) + 2) & 7) + (used & 1), used)
            want = jnp.broadcast_to(used, (1, blk))
            pick = jnp.zeros((p_all, blk), f32)
            for i in range(len(parts) * qb):
                pick = jnp.where(want == i, parts[i // qb][:, (i % qb) * blk:(i % qb + 1) * blk], pick)
            scr[:, q * blk:(q + 1) * blk] = pick
        other = (1 - t) * p_rows
        order = ((other + early, p_rows - early), (t * p_rows, p_rows), (other, early))
        at = 0
        for start, size in order:
            h, l = split(scr[pl.ds(pl.multiple_of(start, 16), size), :])
            out[at:at + size, :] = h
            out[p_all + at:p_all + at + size, :] = l
            at += size

    return pl.pallas_call(
        body, in_specs=[VM] * (len(pieces) + 2), out_specs=VM,
        out_shape=vmem((2 * p_all, ql * blk), bf16),
        scratch_shapes=[pltpu.VMEM((p_all, ql * blk), f32)], name="select", compiler_params=limit(8),
    )(*pieces, q_list, q_count)


def multiply(chosen, t_parts, p_rows, part):
    p_all = chosen.shape[0] // 2
    cols = t_parts[0][0].shape[1]
    ct = cols * len(t_parts) // LANES
    sub = 512 if cols % 512 == 0 else 256
    far_full = p_rows // SUBL - 2
    own_full = p_all // SUBL - far_full - 1

    def body(c, *refs):
        out_c, out_o = refs[-2:]
        for j in range(cols * len(t_parts) // sub):
            which = j * sub // cols
            hi, lo = refs[2 * which:2 * which + 2]
            at = pl.ds(j * sub - which * cols, sub)
            big = jnp.dot(c[...], hi[:, at], preferred_element_type=f32)
            val = big[:p_all] + big[p_all:] + jnp.dot(c[:p_all, :], lo[:, at], preferred_element_type=f32)
            for k in range(sub // LANES):
                jt = j * (sub // LANES) + k
                for i in range(p_all // SUBL):
                    v = val[i * SUBL:(i + 1) * SUBL, k * LANES:(k + 1) * LANES]
                    if i < far_full:
                        out_c[pl.ds((i * ct + jt) * SUBL, SUBL), :] = v
                    elif i < far_full + own_full:
                        out_o[pl.ds(((i - far_full) * ct + jt) * SUBL, SUBL), :] = v
                    else:
                        out_o[pl.ds(own_full * ct * SUBL + jt * part, part), :] = v[:part]
                        rest = SUBL - part
                        if rest:
                            out_c[pl.ds(far_full * ct * SUBL + jt * rest, rest), :] = v[part:]

    return pl.pallas_call(
        body, in_specs=[VM] * (1 + 2 * len(t_parts)), out_specs=[VM, VM],
        out_shape=[vmem(((far_full * SUBL + SUBL - part) * ct, LANES), f32),
                   vmem(((own_full * SUBL + part) * ct, LANES), f32)],
        name="multiply", compiler_params=limit(8),
    )(chosen, *[x for part in t_parts for x in part])


def contract_into(x, rows, ct, n_parts, n_rows, left):
    lane = lax.broadcasted_iota(jnp.int32, (ct, LANES), 1)
    low = lane < LANES // 2
    tail = rows % SUBL

    def row(q):
        per = SUBL if q < rows - tail else tail
        return x[pl.ds((q // SUBL) * ct * SUBL + q % SUBL, ct, stride=per), :]

    for p in range(0, rows, 2):
        a, b = row(p), row(p + 1)
        even = jnp.where(low, a, pltpu.roll(b, LANES // 2, 1))
        odd = jnp.where(low, pltpu.roll(a, LANES // 2, 1), b)
        at = pl.ds((p // 2) * LANES, LANES)
        for i, v in enumerate((even, odd)):
            h, l = split(v)
            left[pl.ds(i * ct, ct), at] = h
            left[pl.ds((2 + i) * ct, ct), at] = l
    half = LANES // 2
    total = None
    at = 0
    for (w_hi, w_lo), (start, count) in zip(n_parts, n_rows):
        k = pl.ds(at * half, count * half)
        w = pl.ds(start * half, count * half)
        both = jnp.dot(left[:, k], w_hi[w, :], preferred_element_type=f32)
        v = both[:2 * ct] + both[2 * ct:]
        v += jnp.dot(left[:2 * ct, k], w_lo[w, :], preferred_element_type=f32)
        total = v if total is None else total + v
        at += count
    return total


def contract(stretches, rows, saved, n_rows, band, sizes, after=()):
    wide = -(-band // LANES)
    cts = [x.shape[0] // rows for x in stretches]
    flat = [w for pair in saved for w in pair]

    def body(*refs):
        refs = list(refs)
        xs = [refs.pop(0) for _ in stretches]
        ws = [refs.pop(0) for _ in flat]
        del refs[:len(after)]
        outs = [refs.pop(0) for _ in sizes]
        acc = refs.pop(0)
        pairs = list(zip(ws[0::2], ws[1::2]))
        base = 0
        for i, (x, ct) in enumerate(zip(xs, cts)):
            val = contract_into(x, rows, ct, pairs, n_rows, refs[i])
            for par in range(2):
                for c in range(wide):
                    acc[c, pl.ds(base + par, ct, stride=2), :] = val[par * ct:(par + 1) * ct, c * LANES:(c + 1) * LANES]
            base += 2 * ct
        at = 0
        for out, size in zip(outs, sizes):
            half = size // 2
            low = lax.broadcasted_iota(jnp.int32, (half, LANES), 1) < LANES // 2
            out[:size, :] = acc[0, at:at + size, :]
            out[size:, :] = jnp.where(low, acc[1, at:at + half, :], pltpu.roll(acc[1, at + half:at + size, :], LANES // 2, 1))
            at += size

    scratch = [pltpu.VMEM((wide, 2 * sum(cts), LANES), f32)]
    for x, ct in zip(stretches, cts):
        scratch.append(pltpu.VMEM((4 * ct, rows * LANES // 2), bf16))
    return pl.pallas_call(
        body, in_specs=[VM] * (len(stretches) + len(flat) + len(after)), out_specs=[VM] * len(sizes),
        out_shape=[vmem((size * band // LANES, LANES), f32) for size in sizes], scratch_shapes=scratch,
        name="contract", compiler_params=limit(12),
    )(*stretches, *flat, *after)


def unpack(x, size, band):
    low = x[size:]
    tail = jnp.concatenate([low, pltpu.roll(low, LANES // 2, 1)], axis=0)
    return jnp.concatenate([x[:size], tail], axis=1)[:, :band]


def gather(rest, oa, ob, oc, ra, rb, orb, band):
    def body(h, a, b, c, d, e, out):
        first = lax.axis_index("tens") == 0
        lower = jnp.where(first, b[...], a[...]) + jnp.where(first, d[...], e[...])
        upper = jnp.where(first, a[...], b[...]) + jnp.where(first, e[...], d[...])
        x, y = h[...], c[...]
        size = x.shape[0] * LANES // band
        x, y = unpack(jnp.where(first, x, y), size, band), unpack(jnp.where(first, y, x), size, band)
        lower, upper = unpack(lower, orb, band), unpack(upper, orb, band)
        zero = jnp.zeros((orb, orb), f32)
        out[...] = (jnp.concatenate([lower, zero, zero], axis=1)
                    + jnp.concatenate([zero, jnp.concatenate([x, y], axis=0), zero], axis=1)
                    + jnp.concatenate([zero, zero, upper], axis=1))

    return pl.pallas_call(
        body, in_specs=[VM] * 6, out_specs=VM, out_shape=vmem((orb, band + 2 * orb), f32),
        name="gather", compiler_params=limit(8),
    )(rest, oa, ob, oc, ra, rb)


def finish(early, mine, other, orb, band):
    def body(e, hr, rc, out):
        first = lax.axis_index("tens") == 0
        x, y = rc[...], hr[...]
        size = x.shape[0] * LANES // band
        x, y = unpack(jnp.where(first, x, y), size, band), unpack(jnp.where(first, y, x), size, band)
        zero = jnp.zeros((orb, orb), f32)
        out[...] = e[...] + jnp.concatenate([zero, jnp.concatenate([x, y], axis=0), zero], axis=1)

    return pl.pallas_call(
        body, in_specs=[VM] * 3, out_specs=VM,
        out_shape=jax.ShapeDtypeStruct((orb, band + 2 * orb), f32), name="finish", compiler_params=limit(4),
    )(early, mine, other)


def paired(chibar, t_blocks, n_saved, q_list, q_count):
    p_rows, n_cols = n_saved.shape
    orb = LANES // 2
    band = n_cols // orb
    nu_t = t_blocks.shape[1] // orb
    part = EARLY_PART
    early = SUBL + part
    cross = p_rows - early
    swap = [(0, 1), (1, 0)]

    n_saved = pltpu.with_memory_space_constraint(n_saved, pltpu.HBM)
    t_blocks = pltpu.with_memory_space_constraint(t_blocks, pltpu.HBM)
    n_far = lax.ppermute(head(n_saved, part), "tens", swap)
    pieces = neighbours(chibar)
    rest = nu_t - orb
    half = orb * orb // 2
    t_main = [prep_t(t_blocks, 0, rest * orb, half, q_count)]
    t_main.append(prep_t(t_blocks, half, rest * orb, half))
    chosen = select(pieces, q_list, q_count, p_rows, 2 * SUBL)
    far_main, own_main = multiply(chosen, t_main, p_rows, part)
    far_main = lax.ppermute(far_main, "tens", swap)
    t_rest = prep_t(t_blocks, orb * orb, -orb * orb, rest * orb)
    far_rest, own_rest = multiply(chosen, [t_rest], p_rows, part)
    far_rest = lax.ppermute(far_rest, "tens", swap)

    near = prep_n(n_saved, orb)
    beyond = prep_far(n_far, part, orb)
    far_rows = [(2 * SUBL, p_rows - 2 * SUBL), (early, SUBL - part)][:2 if part < SUBL else 1]
    o_main, o_rest = contract([own_main, own_rest], p_rows + early, [near, beyond], [(0, p_rows), (0, early)],
                              band, [orb, rest])
    oa = send(o_main, lambda t, s: (t, s - 1 + 2 * t))
    ob = send(o_main, lambda t, s: (1 - t, s - 1 + 2 * t))
    oc = send(o_rest, lambda t, s: (1 - t, s))
    r_main, = contract([far_main], cross, [near, near], far_rows, band, [orb], after=(o_rest,))
    ra = send(r_main, lambda t, s: (t, s + 1 - 2 * t))
    rb = send(r_main, lambda t, s: (1 - t, s + 1 - 2 * t))
    r_rest, = contract([far_rest], cross, [near, near], far_rows, band, [rest])
    rc = send(r_rest, lambda t, s: (1 - t, s))
    early_sum = gather(o_rest, oa, ob, oc, ra, rb, orb, band)
    return finish(early_sum, r_rest, rc, orb, band)


def general(chibar, t_blocks, n_saved, q_list, q_count):
    tens = lax.axis_size("tens")
    t = lax.axis_index("tens")
    p_rows, n_cols = n_saved.shape
    blk = t_blocks.shape[0] // q_list.shape[-1]
    ql = q_list.shape[-1]
    qb = chibar.shape[1] // blk
    reach = REACH
    orb = int(round((n_cols // 3) ** 0.5))
    band = 3 * orb
    nu_t = t_blocks.shape[1] // orb
    high = lax.Precision.HIGH
    slot_ids = q_list.reshape(ql)
    in_use = q_count.reshape(())
    keeper = jnp.arange(ql) < in_use

    def chosen_of(r):
        rows = lax.dynamic_slice_in_dim(chibar, ((t + r) % tens) * p_rows, p_rows, 0)
        pieces = [rows if o == 0 else shift(rows, -o) for o in range(-reach, reach + 1)]
        blocks = [pc[:, b * blk:(b + 1) * blk] for pc in pieces for b in range(qb)]
        out = []
        for q in range(ql):
            pick = blocks[0]
            for i in range(1, len(blocks)):
                pick = jnp.where(slot_ids[q] == i, blocks[i], pick)
            out.append(jnp.where(keeper[q], pick, 0.0))
        return jnp.concatenate(out, axis=1)

    saved = n_saved.reshape(p_rows, orb, band)
    parts = []
    mb = []
    for r in list(range(1, tens)) + [0]:
        m = jnp.dot(chosen_of(r), t_blocks, precision=high, preferred_element_type=jnp.float32)
        if r:
            m = lax.ppermute(m, "tens", [(i, (i + r) % tens) for i in range(tens)])
        mb.append(m)
    mb = [mb[-1]] + mb[:-1]
    for r in range(tens):
        parts.append(jnp.einsum("pnm,pml->nl", mb[r].reshape(p_rows, nu_t, orb), saved, precision=high,
                                preferred_element_type=jnp.float32))
    stacked = jnp.stack(parts)
    order = (t - jnp.arange(tens)) % tens
    if tens == 2:
        partial = jnp.where(t == 0, stacked, stacked[::-1]).reshape(band, band)
    else:
        partial = jnp.take(stacked, order, axis=0).reshape(band, band)
    blocks = partial.reshape(3, orb, band)
    lower = shift(blocks[2], 1)
    upper = shift(blocks[0], -1)
    pad = lambda x, o: jnp.pad(x, ((0, 0), (o * orb, (2 - o) * orb)))
    res = pad(lower, 0) + pad(blocks[1], 1) + pad(upper, 2)
    if tens == 2:
        return res + lax.ppermute(res, "tens", [(0, 1), (1, 0)])
    return lax.psum(res, "tens")


def solution(mesh):
    placed = (
        P(None, "atom"),
        P(None, ("tens", "atom")),
        P("tens", "atom"),
        P("tens", "atom", None),
        P("tens", "atom"),
    )

    def program(body):
        return jax.shard_map(body, mesh=mesh, in_specs=placed, out_specs=P("atom", None), check_vma=False)

    if mesh.shape["tens"] != 2 or mesh.shape["atom"] % 2:
        return program(general)

    return program(paired)
```

```python
import jax
import jax.numpy as jnp
from jax import lax
from jax.experimental import pallas as pl
from jax.experimental.pallas import tpu as pltpu
from jax.sharding import PartitionSpec as P


LANES = 128
SUBL = 8
REACH = 3
EARLY_PART = 8
VM = pl.BlockSpec(memory_space=pltpu.VMEM)
HB = pl.BlockSpec(memory_space=pltpu.HBM)
f32 = jnp.float32
bf16 = jnp.bfloat16


def limit(mib):
    return pltpu.CompilerParams(vmem_limit_bytes=mib * 2**20)


def vmem(shape, dtype):
    return pltpu.VMEM(shape, dtype)


def split(x):
    hi = x.astype(bf16)
    return hi, (x - hi.astype(f32)).astype(bf16)


def shift(x, by):
    atoms = lax.axis_size("atom")
    return lax.ppermute(x, "atom", [(i, (i + by) % atoms) for i in range(atoms)])


def send(x, to):
    atoms = lax.axis_size("atom")
    pairs = []
    for t in range(2):
        for s in range(atoms):
            u, v = to(t, s)
            pairs.append((t * atoms + s, u * atoms + v % atoms))
    return lax.ppermute(x, ("tens", "atom"), pairs)


def neighbours(x):
    atoms = lax.axis_size("atom")
    pair = [(i, i ^ 1) for i in range(atoms)]

    def move(y, pairs):
        return lax.ppermute(y, "atom", pairs)

    far = move(x, [(i, (i + (3 if i % 2 else -3)) % atoms) for i in range(atoms)])
    below = move(x, [(i, (i + 2) % atoms) for i in range(atoms)])
    above = move(x, [(i, (i - 2) % atoms) for i in range(atoms)])
    partner = move(x, pair)
    return [far, below, move(below, pair), x, partner, above, move(above, pair)]


def prep_t(t_blocks, first, slope, cols, *early):
    rows = t_blocks.shape[0]
    step = 64
    sub = 512 if cols % 512 == 0 else LANES

    def body(src, *refs):
        hi, lo, buf, sems = refs[len(early):]
        start = pl.multiple_of(first + slope * lax.axis_index("tens"), LANES)
        copies = []
        for i in range(rows // step):
            here = pl.ds(i * step, step)
            copies.append(pltpu.make_async_copy(src.at[here, pl.ds(start, cols)], buf.at[here], sems.at[i]))
            copies[-1].start()
        for i in range(rows // step):
            copies[i].wait()

            def tile(c, carry, i=i):
                at = pl.ds(pl.multiple_of(c * sub, sub), sub)
                here = pl.ds(i * step, step)
                h, l = split(buf[here, at])
                hi[here, at] = h
                lo[here, at] = l
                return carry

            lax.fori_loop(0, cols // sub, tile, 0)

    return pl.pallas_call(
        body, in_specs=[HB] + [VM] * len(early), out_specs=[VM, VM],
        out_shape=[vmem((rows, cols), bf16), vmem((rows, cols), bf16)],
        scratch_shapes=[pltpu.VMEM((rows, cols), f32), pltpu.SemaphoreType.DMA((rows // step,))],
        name="prep_t", compiler_params=limit(12),
    )(t_blocks, *early)


def head(x, part):
    tiles = x.shape[1] // LANES
    rows = 2 * SUBL

    def body(src, out, buf, sems):
        copies = [pltpu.make_async_copy(src.at[pl.ds(i * SUBL, SUBL)], buf.at[pl.ds(i * SUBL, SUBL)], sems.at[i])
                  for i in range(2)]
        for copy in copies:
            copy.start()
        copies[0].wait()
        for c in range(tiles):
            out[pl.ds(c * SUBL, SUBL), :] = buf[:SUBL, pl.ds(c * LANES, LANES)]
        copies[1].wait()
        for c in range(tiles):
            out[pl.ds(tiles * SUBL + c * part, part), :] = buf[SUBL:SUBL + part, pl.ds(c * LANES, LANES)]

    return pl.pallas_call(
        body, in_specs=[HB], out_specs=VM, out_shape=vmem((tiles * (SUBL + part), LANES), x.dtype),
        scratch_shapes=[pltpu.VMEM((rows, x.shape[1]), f32), pltpu.SemaphoreType.DMA((2,))],
        name="head", compiler_params=limit(4),
    )(x)


def place_row(tiles, first, per, orb, tmp, hi, lo, at):
    half = LANES // 2
    pairs = orb // 2
    low = lax.broadcasted_iota(jnp.int32, (pairs, LANES), 1) < half
    v = [tiles[pl.ds(first + k * per, pairs, stride=3 * per), :] for k in range(3)]
    w1, w2 = (pltpu.roll(x, half, 1) for x in v[1:])
    tmp[0, pl.ds(0, pairs, stride=2), :] = v[0]
    tmp[1, pl.ds(0, pairs, stride=2), :] = v[1]
    tmp[0, pl.ds(1, pairs, stride=2), :] = jnp.where(low, w1, w2)
    tmp[1, pl.ds(1, pairs, stride=2), :] = w2
    for k in range(2):
        h, l = split(tmp[k])
        hi[at, k * LANES:(k + 1) * LANES] = h
        lo[at, k * LANES:(k + 1) * LANES] = l


def prep_n(saved, orb):
    rows, cols = saved.shape
    groups = rows // SUBL

    def body(src, hi, lo, buf, tiles, tmp, sems):
        def copy(i):
            here = pl.ds(pl.multiple_of(i * SUBL, SUBL), SUBL)
            return pltpu.make_async_copy(src.at[here], buf.at[here], sems.at[i])

        for i in range(groups):
            copy(i).start()

        def group(i, carry):
            copy(i).wait()
            here = pl.ds(pl.multiple_of(i * SUBL, SUBL), SUBL)
            for c in range(cols // LANES):
                tiles[c * SUBL:(c + 1) * SUBL, :] = buf[here, c * LANES:(c + 1) * LANES]
            for r in range(SUBL):
                at = pl.ds(pl.multiple_of(i * SUBL * orb + r * orb, orb), orb)
                place_row(tiles, r, SUBL, orb, tmp.at[r], hi, lo, at)
            return carry

        lax.fori_loop(0, groups, group, 0)

    return pl.pallas_call(
        body, in_specs=[HB], out_specs=[VM, VM],
        out_shape=[vmem((rows * orb, 2 * LANES), bf16)] * 2,
        scratch_shapes=[pltpu.VMEM((rows, cols), f32), pltpu.VMEM((cols // LANES * SUBL, LANES), f32),
                        pltpu.VMEM((SUBL, 2, orb, LANES), f32), pltpu.SemaphoreType.DMA((groups,))],
        name="prep_n", compiler_params=limit(10),
    )(saved)


def prep_far(packed, part, orb):
    rows = SUBL + part
    tiles = packed.shape[0] // rows

    def body(src, hi, lo, tmp):
        for p in range(rows):
            first, per = (p, SUBL) if p < SUBL else (tiles * SUBL + p - SUBL, part)
            place_row(src, first, per, orb, tmp.at[p], hi, lo, pl.ds(p * orb, orb))

    return pl.pallas_call(
        body, in_specs=[VM], out_specs=[VM, VM], out_shape=[vmem((rows * orb, 2 * LANES), bf16)] * 2,
        scratch_shapes=[pltpu.VMEM((rows, 2, orb, LANES), f32)], name="prep_far", compiler_params=limit(6),
    )(packed)


def select(pieces, q_list, q_count, p_rows, early):
    p_all, width = pieces[0].shape
    ql = q_list.shape[-1]
    blk = LANES
    qb = width // blk

    def body(*refs):
        parts, (list_ref, count_ref, out, scr) = refs[:len(pieces)], refs[len(pieces):]
        t = lax.axis_index("tens")
        s = lax.axis_index("atom")
        for q in range(ql):
            used = jnp.where(count_ref[...] > q, list_ref[0][:, q:q + 1], -1)
            turned = (((used >> 1) & 1) == 0) & (s % 2 == 1)
            used = jnp.where(turned, 2 * (((used >> 1) + 2) & 7) + (used & 1), used)
            want = jnp.broadcast_to(used, (1, blk))
            pick = jnp.zeros((p_all, blk), f32)
            for i in range(len(parts) * qb):
                pick = jnp.where(want == i, parts[i // qb][:, (i % qb) * blk:(i % qb + 1) * blk], pick)
            scr[:, q * blk:(q + 1) * blk] = pick
        other = (1 - t) * p_rows
        order = ((other + early, p_rows - early), (t * p_rows, p_rows), (other, early))
        at = 0
        for start, size in order:
            h, l = split(scr[pl.ds(pl.multiple_of(start, 16), size), :])
            out[at:at + size, :] = h
            out[p_all + at:p_all + at + size, :] = l
            at += size

    return pl.pallas_call(
        body, in_specs=[VM] * (len(pieces) + 2), out_specs=VM,
        out_shape=vmem((2 * p_all, ql * blk), bf16),
        scratch_shapes=[pltpu.VMEM((p_all, ql * blk), f32)], name="select", compiler_params=limit(8),
    )(*pieces, q_list, q_count)


def multiply(chosen, t_parts, p_rows, part):
    p_all = chosen.shape[0] // 2
    cols = t_parts[0][0].shape[1]
    ct = cols * len(t_parts) // LANES
    sub = 512 if cols % 512 == 0 else 256
    far_full = p_rows // SUBL - 2
    own_full = p_all // SUBL - far_full - 1

    def body(c, *refs):
        out_c, out_o = refs[-2:]
        for j in range(cols * len(t_parts) // sub):
            which = j * sub // cols
            hi, lo = refs[2 * which:2 * which + 2]
            at = pl.ds(j * sub - which * cols, sub)
            big = jnp.dot(c[...], hi[:, at], preferred_element_type=f32)
            val = big[:p_all] + big[p_all:] + jnp.dot(c[:p_all, :], lo[:, at], preferred_element_type=f32)
            for k in range(sub // LANES):
                jt = j * (sub // LANES) + k
                for i in range(p_all // SUBL):
                    v = val[i * SUBL:(i + 1) * SUBL, k * LANES:(k + 1) * LANES]
                    if i < far_full:
                        out_c[pl.ds((i * ct + jt) * SUBL, SUBL), :] = v
                    elif i < far_full + own_full:
                        out_o[pl.ds(((i - far_full) * ct + jt) * SUBL, SUBL), :] = v
                    else:
                        out_o[pl.ds(own_full * ct * SUBL + jt * part, part), :] = v[:part]
                        rest = SUBL - part
                        if rest:
                            out_c[pl.ds(far_full * ct * SUBL + jt * rest, rest), :] = v[part:]

    return pl.pallas_call(
        body, in_specs=[VM] * (1 + 2 * len(t_parts)), out_specs=[VM, VM],
        out_shape=[vmem(((far_full * SUBL + SUBL - part) * ct, LANES), f32),
                   vmem(((own_full * SUBL + part) * ct, LANES), f32)],
        name="multiply", compiler_params=limit(8),
    )(chosen, *[x for part in t_parts for x in part])


def contract_into(x, rows, ct, n_parts, n_rows, left):
    lane = lax.broadcasted_iota(jnp.int32, (ct, LANES), 1)
    low = lane < LANES // 2
    tail = rows % SUBL

    def row(q):
        per = SUBL if q < rows - tail else tail
        return x[pl.ds((q // SUBL) * ct * SUBL + q % SUBL, ct, stride=per), :]

    for p in range(0, rows, 2):
        a, b = row(p), row(p + 1)
        even = jnp.where(low, a, pltpu.roll(b, LANES // 2, 1))
        odd = jnp.where(low, pltpu.roll(a, LANES // 2, 1), b)
        at = pl.ds((p // 2) * LANES, LANES)
        for i, v in enumerate((even, odd)):
            h, l = split(v)
            left[pl.ds(i * ct, ct), at] = h
            left[pl.ds((2 + i) * ct, ct), at] = l
    half = LANES // 2
    total = None
    at = 0
    for (w_hi, w_lo), (start, count) in zip(n_parts, n_rows):
        k = pl.ds(at * half, count * half)
        w = pl.ds(start * half, count * half)
        both = jnp.dot(left[:, k], w_hi[w, :], preferred_element_type=f32)
        v = both[:2 * ct] + both[2 * ct:]
        v += jnp.dot(left[:2 * ct, k], w_lo[w, :], preferred_element_type=f32)
        total = v if total is None else total + v
        at += count
    return total


def contract(stretches, rows, saved, n_rows, band, sizes, after=()):
    wide = -(-band // LANES)
    cts = [x.shape[0] // rows for x in stretches]
    flat = [w for pair in saved for w in pair]

    def body(*refs):
        refs = list(refs)
        xs = [refs.pop(0) for _ in stretches]
        ws = [refs.pop(0) for _ in flat]
        del refs[:len(after)]
        outs = [refs.pop(0) for _ in sizes]
        acc = refs.pop(0)
        pairs = list(zip(ws[0::2], ws[1::2]))
        base = 0
        for i, (x, ct) in enumerate(zip(xs, cts)):
            val = contract_into(x, rows, ct, pairs, n_rows, refs[i])
            for par in range(2):
                for c in range(wide):
                    acc[c, pl.ds(base + par, ct, stride=2), :] = val[par * ct:(par + 1) * ct, c * LANES:(c + 1) * LANES]
            base += 2 * ct
        at = 0
        for out, size in zip(outs, sizes):
            half = size // 2
            low = lax.broadcasted_iota(jnp.int32, (half, LANES), 1) < LANES // 2
            out[:size, :] = acc[0, at:at + size, :]
            out[size:, :] = jnp.where(low, acc[1, at:at + half, :], pltpu.roll(acc[1, at + half:at + size, :], LANES // 2, 1))
            at += size

    scratch = [pltpu.VMEM((wide, 2 * sum(cts), LANES), f32)]
    for x, ct in zip(stretches, cts):
        scratch.append(pltpu.VMEM((4 * ct, rows * LANES // 2), bf16))
    return pl.pallas_call(
        body, in_specs=[VM] * (len(stretches) + len(flat) + len(after)), out_specs=[VM] * len(sizes),
        out_shape=[vmem((size * band // LANES, LANES), f32) for size in sizes], scratch_shapes=scratch,
        name="contract", compiler_params=limit(12),
    )(*stretches, *flat, *after)


def unpack(x, size, band):
    low = x[size:]
    tail = jnp.concatenate([low, pltpu.roll(low, LANES // 2, 1)], axis=0)
    return jnp.concatenate([x[:size], tail], axis=1)[:, :band]


def finish(own, rec, orb, band):
    def body(ho, oa, ob, oc, hr, ra, rb, rc, out):
        first = lax.axis_index("tens") == 0
        lower = jnp.where(first, ob[...], oa[...]) + jnp.where(first, ra[...], rb[...])
        upper = jnp.where(first, oa[...], ob[...]) + jnp.where(first, rb[...], ra[...])
        x = ho[...] + rc[...]
        y = oc[...] + hr[...]
        rest = x.shape[0] * LANES // band
        x, y = unpack(jnp.where(first, x, y), rest, band), unpack(jnp.where(first, y, x), rest, band)
        lower, upper = unpack(lower, orb, band), unpack(upper, orb, band)
        zero = jnp.zeros((orb, orb), f32)
        out[...] = (jnp.concatenate([lower, zero, zero], axis=1)
                    + jnp.concatenate([zero, jnp.concatenate([x, y], axis=0), zero], axis=1)
                    + jnp.concatenate([zero, zero, upper], axis=1))

    return pl.pallas_call(
        body, in_specs=[VM] * 8, out_specs=VM,
        out_shape=jax.ShapeDtypeStruct((orb, band + 2 * orb), f32), name="finish", compiler_params=limit(8),
    )(*own, *rec)


def paired(chibar, t_blocks, n_saved, q_list, q_count):
    p_rows, n_cols = n_saved.shape
    orb = LANES // 2
    band = n_cols // orb
    nu_t = t_blocks.shape[1] // orb
    part = EARLY_PART
    early = SUBL + part
    cross = p_rows - early
    swap = [(0, 1), (1, 0)]

    n_saved = pltpu.with_memory_space_constraint(n_saved, pltpu.HBM)
    t_blocks = pltpu.with_memory_space_constraint(t_blocks, pltpu.HBM)
    n_far = lax.ppermute(head(n_saved, part), "tens", swap)
    pieces = neighbours(chibar)
    rest = nu_t - orb
    half = orb * orb // 2
    t_main = [prep_t(t_blocks, 0, rest * orb, half, q_count)]
    t_main.append(prep_t(t_blocks, half, rest * orb, half))
    chosen = select(pieces, q_list, q_count, p_rows, 2 * SUBL)
    far_main, own_main = multiply(chosen, t_main, p_rows, part)
    far_main = lax.ppermute(far_main, "tens", swap)
    t_rest = prep_t(t_blocks, orb * orb, -orb * orb, rest * orb)
    far_rest, own_rest = multiply(chosen, [t_rest], p_rows, part)
    far_rest = lax.ppermute(far_rest, "tens", swap)

    near = prep_n(n_saved, orb)
    beyond = prep_far(n_far, part, orb)
    far_rows = [(2 * SUBL, p_rows - 2 * SUBL), (early, SUBL - part)][:2 if part < SUBL else 1]
    o_main, o_rest = contract([own_main, own_rest], p_rows + early, [near, beyond], [(0, p_rows), (0, early)],
                              band, [orb, rest])
    oa = send(o_main, lambda t, s: (t, s - 1 + 2 * t))
    ob = send(o_main, lambda t, s: (1 - t, s - 1 + 2 * t))
    oc = send(o_rest, lambda t, s: (1 - t, s))
    r_main, = contract([far_main], cross, [near, near], far_rows, band, [orb], after=(o_rest,))
    ra = send(r_main, lambda t, s: (t, s + 1 - 2 * t))
    rb = send(r_main, lambda t, s: (1 - t, s + 1 - 2 * t))
    r_rest, = contract([far_rest], cross, [near, near], far_rows, band, [rest])
    rc = send(r_rest, lambda t, s: (1 - t, s))
    return finish((o_rest, oa, ob, oc), (r_rest, ra, rb, rc), orb, band)


def general(chibar, t_blocks, n_saved, q_list, q_count):
    tens = lax.axis_size("tens")
    t = lax.axis_index("tens")
    p_rows, n_cols = n_saved.shape
    blk = t_blocks.shape[0] // q_list.shape[-1]
    ql = q_list.shape[-1]
    qb = chibar.shape[1] // blk
    reach = REACH
    orb = int(round((n_cols // 3) ** 0.5))
    band = 3 * orb
    nu_t = t_blocks.shape[1] // orb
    high = lax.Precision.HIGH
    slot_ids = q_list.reshape(ql)
    in_use = q_count.reshape(())
    keeper = jnp.arange(ql) < in_use

    def chosen_of(r):
        rows = lax.dynamic_slice_in_dim(chibar, ((t + r) % tens) * p_rows, p_rows, 0)
        pieces = [rows if o == 0 else shift(rows, -o) for o in range(-reach, reach + 1)]
        blocks = [pc[:, b * blk:(b + 1) * blk] for pc in pieces for b in range(qb)]
        out = []
        for q in range(ql):
            pick = blocks[0]
            for i in range(1, len(blocks)):
                pick = jnp.where(slot_ids[q] == i, blocks[i], pick)
            out.append(jnp.where(keeper[q], pick, 0.0))
        return jnp.concatenate(out, axis=1)

    saved = n_saved.reshape(p_rows, orb, band)
    parts = []
    mb = []
    for r in list(range(1, tens)) + [0]:
        m = jnp.dot(chosen_of(r), t_blocks, precision=high, preferred_element_type=jnp.float32)
        if r:
            m = lax.ppermute(m, "tens", [(i, (i + r) % tens) for i in range(tens)])
        mb.append(m)
    mb = [mb[-1]] + mb[:-1]
    for r in range(tens):
        parts.append(jnp.einsum("pnm,pml->nl", mb[r].reshape(p_rows, nu_t, orb), saved, precision=high,
                                preferred_element_type=jnp.float32))
    stacked = jnp.stack(parts)
    order = (t - jnp.arange(tens)) % tens
    if tens == 2:
        partial = jnp.where(t == 0, stacked, stacked[::-1]).reshape(band, band)
    else:
        partial = jnp.take(stacked, order, axis=0).reshape(band, band)
    blocks = partial.reshape(3, orb, band)
    lower = shift(blocks[2], 1)
    upper = shift(blocks[0], -1)
    pad = lambda x, o: jnp.pad(x, ((0, 0), (o * orb, (2 - o) * orb)))
    res = pad(lower, 0) + pad(blocks[1], 1) + pad(upper, 2)
    if tens == 2:
        return res + lax.ppermute(res, "tens", [(0, 1), (1, 0)])
    return lax.psum(res, "tens")


def solution(mesh):
    placed = (
        P(None, "atom"),
        P(None, ("tens", "atom")),
        P("tens", "atom"),
        P("tens", "atom", None),
        P("tens", "atom"),
    )

    def program(body):
        return jax.shard_map(body, mesh=mesh, in_specs=placed, out_specs=P("atom", None), check_vma=False)

    if mesh.shape["tens"] != 2 or mesh.shape["atom"] % 2:
        return program(general)

    return program(paired)
```
